256 devices in a mesh: section: 2 (over core), dp: 4 (over x), mp: 32 (over z, y).
Axes of the slice: x: 4, y: 4, z: 8, core: 2. Of those that a mesh axis runs over, the one named last changes fastest.
Arguments:
- hidden_in: bfloat16 [2, 384, 8192], P('section', 'dp', 'mp'), may hold values from -6 to 6
- layer_gain: float32 [1, 2, 8192], P(None, 'section'), may hold values from 0.5 to 1.5
- gate_proj: bfloat16 [1, 2, 8192, 16384], P(None, 'section', 'dp', 'mp'), may hold values from -0.0625 to 0.0625
- up_proj: bfloat16 [1, 2, 8192, 16384], P(None, 'section', 'dp', 'mp'), may hold values from -0.0625 to 0.0625
- down_proj: bfloat16 [1, 2, 16384, 8192], P(None, 'section', 'mp', 'dp'), may hold values from -0.046875 to 0.046875
- final_gain: float32 [8192], P('mp'), may hold values from 0.5 to 1.5
- teacher_rows: bfloat16 [2, 4, 192, 8192], P('section', 'dp', None, 'mp'), may hold values from -6 to 6
- send_counts: int32 [2, 4, 4], P('section', 'dp'), may hold values from 0 to 48, as said below
- doc_ids: int32 [2, 4, 96], P('section', 'dp'), may hold values from 0 to 7, never falling along the last dimension, each value on 1 to 24 neighbouring positions
Outputs:
- d_hidden: float32 [2, 384, 8192], P('section', 'dp', 'mp')
- doc_loss: float32 [2, 4], P('section', 'dp')
The draws below stay inside these ranges and needn't reach their ends.
Inputs may be any that keep to these rules, and one draw needn't show every extreme that they name: For every micro-batch m and data group p the counts send_counts[m, q, p] over the 4 teacher shards q sum to exactly 96; in every such column some count equals 48. `doc_ids`: within each micro-batch of each data group the ids never fall, all 8 documents occur, each with 1 to 24 tokens, and one has exactly 24.
All inputs are finite; a program needn't handle non-finite values.
Results may differ from the reference program's by a relative error of at most 0.02.
Values may be sent and summed in bfloat16 or wider, within the bound.
A program may use at most 128 MiB of HBM per device.

```python
import math
import jax
import jax.numpy as jnp
import numpy as np
from jax import lax

D = 8192
FF = 16384
REP = 1
DOCS = 8
TOK = 96
MICRO = 2
ROWS = 384
CAP = 48
DOC_MOST = 24
N_SECTION = 2
N_DP = 4
N_MP = 32


def draw_send_counts(key, part):
    half_cap = CAP // 2
    pair_count = N_DP // 2
    key_spread, key_pick, key_sign = jax.random.split(key, 3)
    spread = jax.random.randint(key_spread, (MICRO, pair_count, N_DP), -half_cap, half_cap + 1)
    chosen = jax.random.randint(key_pick, (MICRO, 1, N_DP), 0, pair_count)
    sign_flip = jax.random.randint(key_sign, (MICRO, 1, N_DP), 0, 2) * 2 - 1
    spread = jnp.where(jnp.arange(pair_count)[None, :, None] == chosen, half_cap * sign_flip, spread)
    stacked = jnp.stack([half_cap + spread, half_cap - spread], axis=2)
    return stacked.reshape(MICRO, N_DP, N_DP).astype(jnp.int32)


def block_levels(key, shape, pieces, least, high):
    factor_of = 1.0
    for position, parts in pieces:
        heights = jax.random.uniform(jax.random.fold_in(jax.random.fold_in(key, 6), position), (parts,), jnp.float32, least / len(pieces), high / len(pieces))
        factor_of = factor_of * jnp.repeat(jnp.exp(heights), shape[position] // parts).reshape((-1,) + (1,) * (len(shape) - 1 - position))
    return factor_of


def length_profile(count, total, most, lean):
    loads = [(1 << 20) // math.isqrt(standing ** lean) + 1 for standing in range(2, count + 1)]
    spare, given = total - most - (count - 1), [1] * (count - 1)
    while spare > 0:
        movable = [i for i in range(count - 1) if given[i] < most]
        whole, budget = sum([loads[i] for i in movable]), spare
        for i in movable:
            extra = min(most - given[i], max(1, budget * loads[i] // whole), spare)
            given[i] = given[i] + extra
            spare = spare - extra
    return np.array([most] + given)


def ragged_sizes(key, number_of, total, most, lean):
    if number_of == 2:
        one = jax.random.randint(key, (), max(1, total - most), min(most, total - 1) + 1)
        return jnp.stack([one, total - one])
    lengths = jnp.asarray(length_profile(number_of, total, most, lean), jnp.int32)
    pairs = (number_of - 1) // 2
    giver, taker = lengths[1:1 + 2 * pairs:2], lengths[2:2 + 2 * pairs:2]
    room = jnp.minimum(giver - 1, most - taker)
    passed = jax.random.randint(jax.random.fold_in(key, 1), (pairs,), 0, 1 << 20) % (room + 1)
    lengths = lengths.at[1:1 + 2 * pairs:2].set(giver - passed).at[2:2 + 2 * pairs:2].set(taker + passed)
    return lengths[jax.random.permutation(jax.random.fold_in(key, 2), number_of)]


def centred(own_key, shape, scale, most, shards=(), held_as=jnp.bfloat16):
    result = scale * jax.random.normal(own_key, shape, jnp.float32)
    if shards:
        result = result * block_levels(own_key, shape, shards, -0.22, 0.18)
    return jnp.clip(result, -most, most).astype(held_as)


def setup_inputs(seed: int = 0) -> dict:
    seeds = jax.random.split(jax.random.key(seed), 10)
    return {
        "hidden_in": centred(seeds[0], (MICRO, ROWS, D), 1.0, 6.0, ((0, 2), (1, 4), (2, 32))),
        "layer_gain": jnp.clip(1.0 + 0.1 * jax.random.normal(seeds[1], (REP, N_SECTION, D), jnp.float32), 0.5, 1.5),
        "gate_proj": centred(seeds[2], (REP, N_SECTION, D, FF), D ** -0.5, 0.0625, ((1, 2), (2, 4), (3, 32))),
        "up_proj": centred(seeds[3], (REP, N_SECTION, D, FF), D ** -0.5, 0.0625, ((1, 2), (2, 4), (3, 32))),
        "down_proj": centred(seeds[4], (REP, N_SECTION, FF, D), FF ** -0.5, 0.046875, ((1, 2), (2, 32), (3, 4))),
        "final_gain": jnp.clip(1.0 + 0.1 * jax.random.normal(seeds[5], (D,), jnp.float32), 0.5, 1.5),
        "teacher_rows": centred(seeds[6], (MICRO, N_DP, N_DP * CAP, D), 1.0, 6.0, ((0, 2), (1, 4), (3, 32))),
        "send_counts": draw_send_counts(jax.random.fold_in(seeds[9], 71), 0),
        "doc_ids": jax.vmap(lambda own: jnp.searchsorted(jnp.cumsum(ragged_sizes(own, DOCS, TOK, DOC_MOST, 1)), jnp.arange(TOK), side="right"))(jax.random.split(seeds[8], MICRO * N_DP)).reshape((MICRO, N_DP, TOK)).astype(jnp.int32),
    }


EPSILON = 1e-05

def feed_forward(carried, gain_row, gate_rows, up_rows, down_rows):
    wide_rows = carried.astype(jnp.float32)
    scale = lax.rsqrt(lax.optimization_barrier(jnp.mean(wide_rows * wide_rows, axis=-1, keepdims=True)) + EPSILON)
    normed = (wide_rows * scale * gain_row[None, :]).astype(jnp.bfloat16)
    gate_full = jnp.dot(normed, gate_rows, preferred_element_type=jnp.float32)
    up_full = jnp.dot(normed, up_rows, preferred_element_type=jnp.float32)
    inner = (jax.nn.silu(gate_full) * up_full).astype(jnp.bfloat16)
    block = FF // N_MP

    def add_block(index, total):
        start = (index * block).astype(jnp.int32)
        piece = lax.dynamic_slice_in_dim(inner, start, block, 1)
        weight_rows = lax.dynamic_slice_in_dim(down_rows, start, block, 0)
        term = jnp.dot(piece, weight_rows, preferred_element_type=jnp.float32).astype(jnp.bfloat16)
        term = lax.optimization_barrier(term)
        return total + term.astype(jnp.float32)
    summed = lax.fori_loop(0, N_MP, add_block, jnp.zeros(wide_rows.shape, jnp.float32))
    return (wide_rows + summed).astype(jnp.bfloat16)

def reference(hidden_in, layer_gain, gate_proj, up_proj, down_proj, final_gain, teacher_rows, send_counts, doc_ids):
    flat_rows = hidden_in.reshape(-1, D)
    for repeat_pos in range(REP):
        for phase_pos in range(N_SECTION):
            flat_rows = feed_forward(flat_rows, layer_gain[repeat_pos, phase_pos], gate_proj[repeat_pos, phase_pos], up_proj[repeat_pos, phase_pos], down_proj[repeat_pos, phase_pos])
    final_rows = flat_rows.reshape(MICRO, N_DP, TOK, D).astype(jnp.float32)
    columns = jnp.transpose(send_counts, (0, 2, 1)).astype(jnp.int32)
    end_rows = jnp.cumsum(columns, axis=-1).astype(jnp.int32)
    starts = (end_rows - columns).astype(jnp.int32)
    positions = jnp.arange(TOK, dtype=jnp.int32)
    source_of = lax.optimization_barrier(jnp.sum((end_rows[:, :, None, :] <= positions[None, None, :, None]).astype(jnp.int32), axis=-1)).astype(jnp.int32)
    first_row = jnp.take_along_axis(starts, source_of, axis=-1).astype(jnp.int32)
    slot_col = (jnp.arange(N_DP, dtype=jnp.int32)[None, :, None] * CAP + positions[None, None, :] - first_row).astype(jnp.int32)
    micro_index = jnp.arange(MICRO, dtype=jnp.int32)[:, None, None]
    targets = teacher_rows[micro_index, source_of, slot_col].astype(jnp.float32)
    member = (doc_ids[..., None] == jnp.arange(DOCS, dtype=jnp.int32)[None, None, None, :]).astype(jnp.float32)
    doc_sizes = lax.optimization_barrier(jnp.sum(member, axis=2))
    row_weight = lax.optimization_barrier(jnp.sum(member * (1.0 / doc_sizes)[:, :, None, :], axis=-1))
    rscale = lax.rsqrt(lax.optimization_barrier(jnp.mean(final_rows * final_rows, axis=-1, keepdims=True)) + EPSILON)
    normal_rows = final_rows * rscale
    student = normal_rows * final_gain
    residual = student - targets
    d_student = row_weight[..., None] * residual
    inner_sum = lax.optimization_barrier(jnp.sum(normal_rows * final_gain * d_student, axis=-1, keepdims=True))
    d_hidden = rscale * (final_gain * d_student - normal_rows * inner_sum / D)
    errors = lax.optimization_barrier(jnp.sum(residual * residual, axis=-1))
    doc_loss = lax.optimization_barrier(jnp.sum(row_weight * 0.5 * errors, axis=-1)) / (DOCS * D)
    return (d_hidden.reshape(MICRO, N_DP * TOK, D), doc_loss)
```

```python
import functools

import jax
import jax.numpy as jnp
from jax import lax
from jax.experimental import pallas as pl
from jax.experimental.pallas import tpu as pltpu
from jax.sharding import PartitionSpec as P

D = 8192
DOCS = 8
EPSILON = 1e-05
NX, NY, NZ = 4, 4, 8
HALF = 48
ROWS = 2 * NX * HALF
FB = 256
FF_LOCAL = 512
DB = 2048
EXTRA = 128
PCOLS = 2 * FF_LOCAL + EXTRA
N_SEMS = 224
MESH = pl.DeviceIdType.MESH
F32 = jnp.float32
BF16 = jnp.bfloat16


class Link:
    def __init__(self, send_sems, recv_sems):
        self.send_sems, self.recv_sems = send_sems, recv_sems
        self.used = 0
        self.sent = []

    def put(self, src, dst, peer):
        i = self.used
        self.used += 1
        copy = pltpu.make_async_remote_copy(
            src_ref=src,
            dst_ref=dst,
            send_sem=self.send_sems.at[i],
            recv_sem=self.recv_sems.at[i],
            device_id=peer,
            device_id_type=MESH,
        )
        copy.start()
        self.sent.append(copy)
        return copy

    def local(self, src, dst):
        i = self.used
        self.used += 1
        copy = pltpu.make_async_copy(src, dst, self.recv_sems.at[i])
        copy.start()
        return copy


def interleave(*steps):
    live = list(steps)
    while live:
        for gen in list(live):
            if next(gen, "end") == "end":
                live.remove(gen)


def kernel(
    hid, tea, cnt, ids, fg, lg, gate, up, down,
    out, loss,
    w1, w2, gains, xs, xn, parts, part_r, inn, terms,
    ya_full, za_r, zb_r, yb_full,
    tea_r, cnt_s, cnt_r, fin, sum_y, sum_z, sq,
    send_sems, recv_sems,
):
    s = lax.axis_index("section")
    x = lax.axis_index("dp")
    m = lax.axis_index("mp")
    y, z = lax.rem(m, NY), lax.div(m, NY)
    a, b = lax.div(z, 2), lax.rem(z, 2)
    o = 1 - s
    link = Link(send_sems, recv_sems)

    def at_y(k):
        return lax.rem(y + k + NY, NY)

    def at_z(k):
        return lax.rem(z + k + NZ, NZ)

    def at_x(k):
        return lax.rem(x + k + NX, NX)

    def peer_y(k):
        return {"mp": z * NY + at_y(k)}

    def peer_z(k):
        return {"mp": at_z(k) * NY + y}

    def peer_x(k):
        return {"dp": at_x(k)}

    core = {"section": o}
    swap = {"dp": a, "mp": (2 * x + b) * NY + y}
    own_side = a == x

    barrier = pltpu.get_barrier_semaphore()
    peers = (
        [peer_y(k) for k in range(1, NY)]
        + [peer_z(k) for k in range(1, NZ)]
        + [peer_x(k) for k in range(1, NX)]
        + [core]
    )
    for peer in peers:
        pl.semaphore_signal(barrier, inc=1, device_id=peer, device_id_type=MESH)

    @pl.when(jnp.logical_not(own_side))
    def _():
        pl.semaphore_signal(barrier, inc=1, device_id=swap, device_id_type=MESH)

    loads = [
        link.local(gate.at[0, 0], w1.at[s, :, pl.ds(0, FF_LOCAL)]),
        link.local(up.at[0, 0], w1.at[s, :, pl.ds(FF_LOCAL, FF_LOCAL)]),
        link.local(down.at[0, 0], w2.at[s]),
        link.local(lg.at[0, :, pl.ds(pl.multiple_of(x * DB, DB), DB)], gains.at[s]),
    ]
    pl.semaphore_wait(barrier, jnp.where(own_side, len(peers), len(peers) + 1))

    def exchange(src, dst):
        i = link.used
        link.used += 1
        remote = pltpu.make_async_remote_copy(
            src_ref=src, dst_ref=dst, send_sem=send_sems.at[i], recv_sem=recv_sems.at[i],
            device_id=swap, device_id_type=MESH,
        )
        here = pltpu.make_async_copy(src, dst, recv_sems.at[i])

        @pl.when(jnp.logical_not(own_side))
        def _():
            remote.start()

        @pl.when(own_side)
        def _():
            here.start()

        def wait():
            @pl.when(jnp.logical_not(own_side))
            def _():
                remote.wait()

            @pl.when(own_side)
            def _():
                here.wait()

        return wait

    swapped = exchange(hid, xs.at[0, :, b, y, x])

    crossing = [
        link.put(lg.at[0, :, pl.ds(pl.multiple_of(x * DB, DB), DB)], gains.at[s], core),
        link.put(gate.at[0, 0], w1.at[s, :, pl.ds(0, FF_LOCAL)], core),
        link.put(up.at[0, 0], w1.at[s, :, pl.ds(FF_LOCAL, FF_LOCAL)], core),
        link.put(down.at[0, 0], w2.at[s], core),
    ]


    def gather_ring4(block, half, pos, peer):
        right = link.put(block(pos(0)), block(pos(0)), peer(1))
        left = link.put(block(pos(0)), block(pos(0)), peer(-1))
        yield
        right.wait_recv()
        right2 = link.put(half(pos(-1), 0), half(pos(-1), 0), peer(1))
        left.wait_recv()
        left2 = link.put(half(pos(1), 1), half(pos(1), 1), peer(-1))
        yield
        right2.wait_recv()
        left2.wait_recv()

    def gather_ring8(block, half):
        right = left = None
        for hop in range(1, 5):
            if right is not None:
                right.wait_recv()
            src = block(at_z(1 - hop)) if hop < 4 else half(at_z(1 - hop), 0)
            right = link.put(src, src, peer_z(1))
            if left is not None:
                left.wait_recv()
            src = block(at_z(hop - 1)) if hop < 4 else half(at_z(hop - 1), 1)
            left = link.put(src, src, peer_z(-1))
            yield
        right.wait_recv()
        left.wait_recv()

    def add_into(dst, got):
        dst[...] = dst[...] + got[...]

    def scatter_ring4(half, pos, peer, slots, add, finish):
        far_r = link.put(half(pos(2), 0), slots(0), peer(1))
        far_l = link.put(half(pos(2), 1), slots(1), peer(-1))
        near_r = link.put(half(pos(1), 1), slots(2), peer(1))
        near_l = link.put(half(pos(-1), 0), slots(3), peer(-1))
        yield
        far_r.wait_recv()
        add(half(pos(1), 0), slots(0))
        last_r = link.put(half(pos(1), 0), slots(4), peer(1))
        far_l.wait_recv()
        add(half(pos(-1), 1), slots(1))
        last_l = link.put(half(pos(-1), 1), slots(5), peer(-1))
        yield
        near_r.wait_recv()
        near_l.wait_recv()
        last_r.wait_recv()
        last_l.wait_recv()
        finish(0, half(pos(0), 0), slots(4), slots(3))
        finish(1, half(pos(0), 1), slots(2), slots(5))

    def scatter_ring8(block, half, slots, slot_half, finish):
        right = link.put(half(at_z(4), 0), slot_half(0, 0), peer_z(1))
        left = link.put(half(at_z(4), 1), slot_half(1, 0), peer_z(-1))
        for hop in range(1, 4):
            yield
            right.wait_recv()
            dest = at_z(4 - hop)
            if hop == 1:
                add_into(half(dest, 0), slot_half(0, 0))
            else:
                add_into(block(dest), slots(0, hop - 1))
            right = link.put(block(dest), slots(0, hop), peer_z(1))
            left.wait_recv()
            dest = at_z(hop - 4)
            if hop == 1:
                add_into(half(dest, 1), slot_half(1, 0))
            else:
                add_into(block(dest), slots(1, hop - 1))
            left = link.put(block(dest), slots(1, hop), peer_z(-1))
        yield
        right.wait_recv()
        left.wait_recv()
        finish(block(z), slots(0, 3), slots(1, 3))


    lanes = (pl.ds(0, 128), pl.ds(128, 128))
    pairs = (pl.ds(0, 2), pl.ds(2, 2))

    def gather_rows_a(l):
        yield from gather_ring8(
            lambda q: xs.at[l, 0, lax.rem(q, 2), y, lax.div(q, 2)],
            lambda q, h: xs.at[l, 0, lax.rem(q, 2), y, lax.div(q, 2), :, lanes[h]],
        )
        yield from gather_ring4(
            lambda q: xs.at[l, 0, :, q],
            lambda q, h: xs.at[l, 0, h, q],
            at_y, peer_y,
        )

    def gather_rows_b(l):
        yield from gather_ring4(
            lambda q: xs.at[l, 1, b, q, a],
            lambda q, h: xs.at[l, 1, b, q, a, :, lanes[h]],
            at_y, peer_y,
        )
        yield from gather_ring8(
            lambda q: xs.at[l, 1, lax.rem(q, 2), :, lax.div(q, 2)],
            lambda q, h: xs.at[l, 1, lax.rem(q, 2), pairs[h], lax.div(q, 2)],
        )

    def widen(l):
        sq[...] = jnp.zeros_like(sq)
        for k in range(8):
            kb, ky = divmod(k, NY)
            value = xs[l, :, kb, ky].reshape(ROWS, FB).astype(F32)
            xn[:, k * FB:(k + 1) * FB] = (value * gains[l, :, k * FB:(k + 1) * FB]).astype(BF16)
            square = value * value
            sq[...] += square[:, :128] + square[:, 128:]

    def split_sum(total):
        wide = jnp.broadcast_to(total, total.shape[:-1] + (EXTRA,))
        head = wide.astype(BF16).astype(F32)
        lane = lax.broadcasted_iota(jnp.int32, wide.shape, wide.ndim - 1)
        return jnp.where(lane < EXTRA // 2, head, wide - head).astype(BF16)

    def join_sum(tile):
        return jnp.sum(tile.astype(F32), axis=-1, keepdims=True) * (2.0 / EXTRA)

    def gate_up(l):
        total = jnp.sum(sq[...], axis=-1, keepdims=True)
        extra = split_sum(total).reshape(2, NX, HALF, EXTRA)
        parts[l, :, :, :, 2 * FF_LOCAL:] = extra
        for n in range(4):
            value = jnp.dot(xn[...], w1[l, :, n * FB:(n + 1) * FB], preferred_element_type=F32)
            parts[l, :, :, :, n * FB:(n + 1) * FB] = value.astype(BF16).reshape(2, NX, HALF, FB)

    def reduce_parts(l):
        def add(dst, got):
            dst[:, :2 * FF_LOCAL] = dst[:, :2 * FF_LOCAL] + got[:, :2 * FF_LOCAL]
            dst[:, 2 * FF_LOCAL:] = split_sum(join_sum(dst[:, 2 * FF_LOCAL:]) + join_sum(got[:, 2 * FF_LOCAL:]))

        def finish(c, mine, one, two):
            squares = (
                join_sum(mine[:, 2 * FF_LOCAL:]) + join_sum(one[:, 2 * FF_LOCAL:]) + join_sum(two[:, 2 * FF_LOCAL:])
            )
            scale = lax.rsqrt(squares / D + EPSILON)

            def total(first):
                cols = slice(first, first + FF_LOCAL)
                return (mine[:, cols].astype(F32) + one[:, cols].astype(F32) + two[:, cols].astype(F32)) * scale

            act = total(0)
            inn[l, c, x] = (act / (1.0 + jnp.exp(-act)) * total(FF_LOCAL)).astype(BF16)

        yield from scatter_ring4(
            lambda q, h: parts.at[l, h, q], at_x, peer_x, lambda i: part_r.at[l, i], add, finish
        )

    def gather_inner(l):
        yield from gather_ring4(
            lambda q: inn.at[l, :, q], lambda q, h: inn.at[l, h, q], at_x, peer_x
        )

    def down_terms(l):
        rows = inn[l].reshape(ROWS, FF_LOCAL)
        for n in range(8):
            nb, ny = divmod(n, NY)
            value = jnp.dot(rows, w2[l, :, n * FB:(n + 1) * FB], preferred_element_type=F32)
            terms[l, :, nb, ny] = value.astype(BF16).reshape(2, NX, HALF, FB)

    def store_next(l, c, value):
        fresh = xs[l, c, b, y, a].astype(F32) + value
        if l == 0:
            xs[1, c, b, y, a] = fresh.astype(BF16)
        else:
            fin[0, c] = fresh.astype(BF16)

    def reduce_terms_a(l):
        def finish_y(h, mine, one, two):
            mine[...] = (mine[...].astype(F32) + one[...].astype(F32) + two[...].astype(F32)).astype(BF16)

        yield from scatter_ring4(
            lambda q, h: terms.at[l, 0, h, q],
            at_y, peer_y,
            lambda i: ya_full.at[l, i], add_into, finish_y,
        )

        def finish_z(mine, one, two):
            store_next(l, 0, mine[...].astype(F32) + one[...].astype(F32) + two[...].astype(F32))

        yield from scatter_ring8(
            lambda q: terms.at[l, 0, lax.rem(q, 2), y, lax.div(q, 2)],
            lambda q, h: terms.at[l, 0, lax.rem(q, 2), y, lax.div(q, 2), :, lanes[h]],
            lambda side, hop: za_r.at[l, side, hop],
            lambda side, hop: za_r.at[l, side, hop, :, lanes[side]],
            finish_z,
        )

    def reduce_terms_b(l):
        def finish_z(mine, one, two):
            mine[...] = (mine[...].astype(F32) + one[...].astype(F32) + two[...].astype(F32)).astype(BF16)

        yield from scatter_ring8(
            lambda q: terms.at[l, 1, lax.rem(q, 2), :, lax.div(q, 2)],
            lambda q, h: terms.at[l, 1, lax.rem(q, 2), pairs[h], lax.div(q, 2)],
            lambda side, hop: zb_r.at[l, side, hop],
            lambda side, hop: zb_r.at[l, side, hop, pairs[side]],
            finish_z,
        )
        done = []

        def finish_y(h, mine, one, two):
            done.append(mine[...].astype(F32) + one[...].astype(F32) + two[...].astype(F32))

        yield from scatter_ring4(
            lambda q, h: terms.at[l, 1, b, q, a, :, lanes[h]],
            at_y, peer_y,
            lambda i: yb_full.at[l, i], add_into, finish_y,
        )
        store_next(l, 1, jnp.concatenate(done, axis=1))


    for p in range(NX):
        cnt_s[p] = jnp.full((8, 128), cnt[0, p], jnp.int32)
    swapped()
    first = gather_rows_a(0), gather_rows_b(0)
    for gen in first:
        next(gen)
    arrivals = []
    for k in range(1, NX):
        arrivals.append(link.put(tea.at[at_x(k)], tea_r.at[x], peer_x(k)))
        arrivals.append(link.put(cnt_s.at[at_x(k)], cnt_r.at[x], peer_x(k)))
    own_rows = link.local(tea.at[x], tea_r.at[x])
    cnt_r[x] = cnt_s[x]
    interleave(*first)

    for l in range(2):
        if l == 0:
            for copy in loads:
                copy.wait()
            for copy in crossing:
                copy.wait_recv()
        else:
            interleave(gather_rows_a(1), gather_rows_b(1))
        widen(l)
        gate_up(l)
        interleave(reduce_parts(l))
        interleave(gather_inner(l))
        down_terms(l)
        interleave(reduce_terms_a(l), reduce_terms_b(l))
    swapped = exchange(fin.at[0], fin.at[1])

    own_rows.wait()
    for copy in arrivals:
        copy.wait_recv()
    n_rows = 2 * HALF
    row = lax.broadcasted_iota(jnp.int32, (n_rows, HALF), 0)
    slot = lax.broadcasted_iota(jnp.int32, (n_rows, HALF), 1)
    start = jnp.zeros((1, HALF), jnp.int32)
    targets = jnp.zeros((n_rows, FB), F32)
    for q in range(NX):
        count = cnt_r[q, 0:1, :HALF]
        chosen = jnp.logical_and(row - start == slot, slot < count)
        targets += jnp.dot(chosen.astype(BF16), tea_r[q], preferred_element_type=F32)
        start = start + count
    ids_row = ids[...].astype(F32)
    row = lax.broadcasted_iota(jnp.int32, (n_rows, n_rows), 0)
    col = lax.broadcasted_iota(jnp.int32, (n_rows, n_rows), 1)
    diagonal = row == col
    ids_col = jnp.sum(jnp.where(diagonal, ids_row, 0.0), axis=1, keepdims=True)
    size = jnp.sum((ids_col == ids_row).astype(F32), axis=1, keepdims=True)
    weight = 1.0 / size

    swapped()
    final = fin[1].reshape(n_rows, FB).astype(F32)
    gain = fg[...]
    gained = final * gain
    columns = [
        jnp.sum(value, axis=1, keepdims=True)
        for value in (final * final, gained * gained, gained * targets, targets * targets)
    ]
    for i, column in enumerate(columns):
        sum_y[y, i:i + 1, :n_rows] = jnp.sum(jnp.where(diagonal, column, 0.0), axis=0, keepdims=True)
    sent = [link.put(sum_y.at[y], sum_y.at[y], peer_y(k)) for k in range(1, NY)]
    for copy in sent:
        copy.wait_recv()
    sum_z[z] = sum_y[0] + sum_y[1] + sum_y[2] + sum_y[3]
    sent = [link.put(sum_z.at[z], sum_z.at[z], peer_z(k)) for k in range(1, NZ)]
    for copy in sent:
        copy.wait_recv()
    sums = sum_z[0]
    for k in range(1, NZ):
        sums = sums + sum_z[k]
    s1, s2, s3, s4 = [
        jnp.sum(jnp.where(diagonal, sums[i:i + 1, :n_rows], 0.0), axis=1, keepdims=True) for i in range(4)
    ]
    rscale = lax.rsqrt(s1 / D + EPSILON)
    inner_sum = weight * (rscale * rscale * s2 - rscale * s3)
    errors = rscale * rscale * s2 - 2.0 * rscale * s3 + s4
    normal = final * rscale
    d_student = weight * (normal * gain - targets)
    out[...] = rscale * (gain * d_student - normal * (inner_sum / D))
    total = jnp.sum(weight * 0.5 * errors, axis=0, keepdims=True) / (DOCS * D)
    loss[...] = total

    for copy in link.sent:
        copy.wait_send()


def body(
    hidden_in, layer_gain, gate_proj, up_proj, down_proj, final_gain, teacher_rows, send_counts, doc_ids
):
    vmem = pl.BlockSpec(memory_space=pltpu.VMEM)
    smem = pl.BlockSpec(memory_space=pltpu.SMEM)
    hbm = pl.BlockSpec(memory_space=pl.ANY)
    scratch = [
        pltpu.VMEM((2, DB, 2 * FF_LOCAL), BF16),
        pltpu.VMEM((2, FF_LOCAL, DB), BF16),
        pltpu.VMEM((2, 1, DB), F32),
        pltpu.VMEM((2, 2, 2, NY, NX, HALF, FB), BF16),
        pltpu.VMEM((ROWS, DB), BF16),
        pltpu.VMEM((2, 2, NX, HALF, PCOLS), BF16),
        pltpu.VMEM((2, 6, HALF, PCOLS), BF16),
        pltpu.VMEM((2, 2, NX, HALF, FF_LOCAL), BF16),
        pltpu.VMEM((2, 2, 2, NY, NX, HALF, FB), BF16),
        pltpu.VMEM((2, 6, NX, HALF, FB), BF16),
        pltpu.VMEM((2, 2, 4, HALF, FB), BF16),
        pltpu.VMEM((2, 2, 4, NY, HALF, FB), BF16),
        pltpu.VMEM((2, 6, HALF, 128), BF16),
        pltpu.VMEM((NX, HALF, FB), BF16),
        pltpu.VMEM((NX, 8, 128), jnp.int32),
        pltpu.VMEM((NX, 8, 128), jnp.int32),
        pltpu.VMEM((2, 2, HALF, FB), BF16),
        pltpu.VMEM((NY, 8, 128), F32),
        pltpu.VMEM((NZ, 8, 128), F32),
        pltpu.VMEM((ROWS, 128), F32),
        pltpu.SemaphoreType.DMA((N_SEMS,)),
        pltpu.SemaphoreType.DMA((N_SEMS,)),
    ]
    grad, loss = pl.pallas_call(
        kernel,
        out_shape=(
            jax.ShapeDtypeStruct((2 * HALF, FB), F32),
            jax.ShapeDtypeStruct((1, 1), F32),
        ),
        in_specs=[vmem, vmem, smem, vmem, vmem, hbm, hbm, hbm, hbm],
        out_specs=(vmem, vmem),
        scratch_shapes=scratch,
        compiler_params=pltpu.CompilerParams(
            collective_id=0, has_side_effects=True, vmem_limit_bytes=56 * 1024 * 1024
        ),
    )(
        hidden_in.reshape(2, HALF, FB),
        teacher_rows.reshape(NX, HALF, FB),
        send_counts.reshape(1, NX),
        doc_ids.reshape(1, 2 * HALF),
        final_gain.reshape(1, FB),
        layer_gain,
        gate_proj,
        up_proj,
        down_proj,
    )
    return grad[None], loss


def solution(mesh):
    in_specs = (
        P("section", "dp", "mp"),
        P(None, "section", None),
        P(None, "section", "dp", "mp"),
        P(None, "section", "dp", "mp"),
        P(None, "section", "mp", "dp"),
        P("mp"),
        P("section", "dp", None, "mp"),
        P("section", "dp", None),
        P("section", "dp", None),
    )
    out_specs = (P("section", "dp", "mp"), P("section", "dp"))
    return jax.shard_map(body, mesh=mesh, in_specs=in_specs, out_specs=out_specs, check_vma=False)
```

```python
import functools

import jax
import jax.numpy as jnp
from jax import lax
from jax.experimental import pallas as pl
from jax.experimental.pallas import tpu as pltpu
from jax.sharding import PartitionSpec as P

D = 8192
DOCS = 8
EPSILON = 1e-05
NX, NY, NZ = 4, 4, 8
HALF = 48
ROWS = 2 * NX * HALF
FB = 256
FF_LOCAL = 512
DB = 2048
EXTRA = 128
PCOLS = 2 * FF_LOCAL + EXTRA
N_SEMS = 224
MESH = pl.DeviceIdType.MESH
ORDER = "001010110010101010101101"
F32 = jnp.float32
BF16 = jnp.bfloat16


class Link:
    def __init__(self, send_sems, recv_sems):
        self.send_sems, self.recv_sems = send_sems, recv_sems
        self.used = 0
        self.sent = []

    def take(self, count=1):
        first = self.used
        self.used += count
        return first

    def make(self, src, dst, peer, send, recv):
        return pltpu.make_async_remote_copy(
            src_ref=src,
            dst_ref=dst,
            send_sem=self.send_sems.at[send],
            recv_sem=self.recv_sems.at[recv],
            device_id=peer,
            device_id_type=MESH,
        )

    def put(self, src, dst, peer):
        i = self.take()
        copy = self.make(src, dst, peer, i, i)
        copy.start()
        self.sent.append((None, copy))
        return copy

    def put_if(self, needed, src, dst, peer, send, recv):
        copy = self.make(src, dst, peer, send, recv)
        pl.when(needed)(lambda: copy.start())
        self.sent.append((needed, copy))

    def local(self, src, dst):
        copy = pltpu.make_async_copy(src, dst, self.recv_sems.at[self.take()])
        copy.start()
        return copy

    def finish(self):
        for needed, copy in self.sent:
            if needed is None:
                copy.wait_send()
            else:
                pl.when(needed)(lambda copy=copy: copy.wait_send())


def drive(order, gens):
    for name in order:
        next(gens[int(name)], None)
    for gen in gens:
        assert next(gen, "end") == "end"


def kernel(
    hid, tea, cnt, ids, fg, lg, gate, up, down,
    out, loss,
    w1, w2, gains, xs, xn, parts, part_r, inn, terms,
    y_r, z_r, kept, last_r,
    tea_r, cnt_s, cnt_r, sum_y, sum_z,
    send_sems, recv_sems,
):
    s = lax.axis_index("section")
    x = lax.axis_index("dp")
    m = lax.axis_index("mp")
    y, z = lax.rem(m, NY), lax.div(m, NY)
    a, b = lax.div(z, 2), lax.rem(z, 2)
    o = 1 - s
    link = Link(send_sems, recv_sems)

    def at_y(k):
        return lax.rem(y + k + NY, NY)

    def at_z(k):
        return lax.rem(z + k + NZ, NZ)

    def at_x(k):
        return lax.rem(x + k + NX, NX)

    def peer_y(k):
        return {"mp": z * NY + at_y(k)}

    def peer_z(k):
        return {"mp": at_z(k) * NY + y}

    def peer_x(k):
        return {"dp": at_x(k)}

    core = {"section": o}
    swap = {"dp": a, "mp": (2 * x + b) * NY + y}
    own_side = a == x
    planes = [{"dp": a, "mp": j * NY + y} for j in range(NZ)]
    homes = [{"dp": j // 2, "mp": (2 * x + j % 2) * NY + y} for j in range(NZ)]

    def other(j):
        return jnp.logical_not(jnp.logical_and(own_side, z == j))

    barrier = pltpu.get_barrier_semaphore()
    peers = (
        [peer_y(k) for k in range(1, NY)]
        + [peer_z(k) for k in range(1, NZ)]
        + [peer_x(k) for k in range(1, NX)]
        + [core]
    )
    for group in (homes, planes):
        for j, peer in enumerate(group):

            @pl.when(other(j))
            def _():
                pl.semaphore_signal(barrier, inc=1, device_id=peer, device_id_type=MESH)

    for peer in peers:
        pl.semaphore_signal(barrier, inc=1, device_id=peer, device_id_type=MESH)

    loads = [
        link.local(gate.at[0, 0], w1.at[s, :, pl.ds(0, FF_LOCAL)]),
        link.local(up.at[0, 0], w1.at[s, :, pl.ds(FF_LOCAL, FF_LOCAL)]),
        link.local(down.at[0, 0], w2.at[s]),
        link.local(lg.at[0, :, pl.ds(pl.multiple_of(x * DB, DB), DB)], gains.at[s]),
    ]
    many = len(peers) + 2 * NZ
    pl.semaphore_wait(barrier, jnp.where(own_side, many - 2, many))

    def spread(group, src, dst, key):
        first = link.take(NZ)
        for j in range(NZ):
            link.put_if(other(j), src(j), dst, group[j], first + j, first + key)
        return first

    def collect(first, ref):
        for j in range(NZ):
            copy = link.make(ref, ref, swap, first + j, first + j)
            pl.when(other(j))(lambda copy=copy: copy.wait_recv())


    def order(n):
        return sorted(range(1, n), key=lambda k: -min(k, n - k))

    def gather_direct(block, pos, peer, n):
        mine = block(pos(0))
        copies = [link.put(mine, mine, peer(k)) for k in order(n)]
        yield
        for copy in copies:
            copy.wait_recv()

    def scatter_direct(block, pos, peer, n, slot, finish):
        copies = [link.put(block(pos(k)), slot(k - 1), peer(k)) for k in order(n)]
        yield
        for copy in copies:
            copy.wait_recv()
        finish(block(pos(0)), [slot(k - 1) for k in range(1, n)])


    def widen(l, c):
        squares = jnp.zeros((ROWS // 2, 128), F32)
        for k in range(8):
            kb, ky = divmod(k, NY)
            value = xs[l, c, kb, ky].reshape(ROWS // 2, FB).astype(F32)
            xn[:, k * FB:(k + 1) * FB] = (value * gains[l, :, k * FB:(k + 1) * FB]).astype(BF16)
            square = value * value
            squares = squares + square[:, :128] + square[:, 128:]
        return jnp.sum(squares, axis=-1, keepdims=True)

    def split_sum(total):
        wide = jnp.broadcast_to(total, total.shape[:-1] + (EXTRA,))
        head = wide.astype(BF16).astype(F32)
        lane = lax.broadcasted_iota(jnp.int32, wide.shape, wide.ndim - 1)
        return jnp.where(lane < EXTRA // 2, head, wide - head).astype(BF16)

    def join_sum(tile):
        return jnp.sum(tile.astype(F32), axis=-1, keepdims=True) * (2.0 / EXTRA)

    def gate_up(l, c):
        extra = split_sum(widen(l, c)).reshape(NX, HALF, EXTRA)
        parts[l, c, :, :, 2 * FF_LOCAL:] = extra
        for n in range(4):
            value = jnp.dot(xn[...], w1[l, :, n * FB:(n + 1) * FB], preferred_element_type=F32)
            parts[l, c, :, :, n * FB:(n + 1) * FB] = value.astype(BF16).reshape(NX, HALF, FB)

    def reduce_parts(l, c):
        def finish(mine, others):
            every = [mine] + others
            squares = sum(join_sum(ref[:, 2 * FF_LOCAL:]) for ref in every)
            scale = lax.rsqrt(squares / D + EPSILON)

            def total(first):
                return sum(ref[:, first:first + FF_LOCAL].astype(F32) for ref in every) * scale

            act = total(0)
            inn[l, c, x] = (act / (1.0 + jnp.exp(-act)) * total(FF_LOCAL)).astype(BF16)

        yield from scatter_direct(
            lambda q: parts.at[l, c, q], at_x, peer_x, NX, lambda i: part_r.at[l, c, i], finish
        )

    def down_terms(l, c):
        rows = inn[l, c].reshape(ROWS // 2, FF_LOCAL)
        for n in range(8):
            nb, ny = divmod(n, NY)
            value = jnp.dot(rows, w2[l, :, n * FB:(n + 1) * FB], preferred_element_type=F32)
            terms[l, c, nb, ny] = value.astype(BF16).reshape(NX, HALF, FB)

    def add_up(mine, others):
        return sum((ref[...].astype(F32) for ref in others), mine[...].astype(F32))

    def sum_terms(mine, others):
        mine[...] = add_up(mine, others).astype(BF16)

    def chain(c):
        landing = xs.at[0, c, b, y, x]
        first = spread(planes, lambda j: hid.at[c], landing, 2 * x + b)

        @pl.when(own_side)
        def _():
            landing[...] = hid[c]

        yield
        collect(first, landing)
        for l in range(2):
            if l == 1:
                yield from gather_direct(
                    lambda q: xs.at[1, c, lax.rem(q, 2), y, lax.div(q, 2)], at_z, peer_z, NZ
                )
            yield from gather_direct(lambda q: xs.at[l, c, :, q], at_y, peer_y, NY)
            if l == 0 and c == 0:
                for copy in loads:
                    copy.wait()
                for copy in crossing:
                    copy.wait_recv()
            gate_up(l, c)
            yield from reduce_parts(l, c)
            yield from gather_direct(lambda q: inn.at[l, c, q], at_x, peer_x, NX)
            down_terms(l, c)
            yield from scatter_direct(
                lambda q: terms.at[l, c, :, q], at_y, peer_y, NY, lambda i: y_r.at[l, c, i], sum_terms
            )
            if l == 0:
                def finish(mine, others):
                    fresh = xs[0, c, b, y, a].astype(F32) + add_up(mine, others)
                    xs[1, c, b, y, a] = fresh.astype(BF16)

                yield from scatter_direct(
                    lambda q: terms.at[0, c, lax.rem(q, 2), y, lax.div(q, 2)],
                    at_z, peer_z, NZ, lambda i: z_r.at[c, i], finish,
                )
                base = link.take()
                link.put_if(
                    jnp.logical_not(own_side), xs.at[1, c, b, y, a], kept.at[c], swap, base, base
                )
                state_sems[c] = base

                @pl.when(own_side)
                def _():
                    kept[c] = xs[1, c, b, y, a]

        first = spread(homes, lambda j: terms.at[1, c, j % 2, y, j // 2], last_r.at[c, z], z)

        @pl.when(own_side)
        def _():
            last_r[c, z] = terms[1, c, b, y, a]

        yield
        collect(first, last_r.at[c, 0])
        copy = link.make(kept.at[c], kept.at[c], swap, state_sems[c], state_sems[c])
        pl.when(jnp.logical_not(own_side))(lambda: copy.wait_recv())
        value = kept[c].astype(F32)
        for j in range(NZ):
            value = value + last_r[c, j].astype(F32)
        finals[c] = value.astype(BF16).astype(F32)

    state_sems, finals = [None, None], [None, None]


    chains = [chain(0), chain(1)]
    next(chains[0])
    next(chains[1])

    gain_block = lg.at[0, :, pl.ds(pl.multiple_of(x * DB, DB), DB)]
    crossing = [
        link.put(gain_block, gains.at[s], core),
        link.put(gate.at[0, 0], w1.at[s, :, pl.ds(0, FF_LOCAL)], core),
        link.put(up.at[0, 0], w1.at[s, :, pl.ds(FF_LOCAL, FF_LOCAL)], core),
        link.put(down.at[0, 0], w2.at[s], core),
    ]

    for p in range(NX):
        cnt_s[p] = jnp.full((8, 128), cnt[0, p], jnp.int32)
    arrivals = []
    for k in range(1, NX):
        arrivals.append(link.put(tea.at[at_x(k)], tea_r.at[x], peer_x(k)))
        arrivals.append(link.put(cnt_s.at[at_x(k)], cnt_r.at[x], peer_x(k)))
    own_rows = link.local(tea.at[x], tea_r.at[x])
    cnt_r[x] = cnt_s[x]

    drive(ORDER, chains)

    own_rows.wait()
    for copy in arrivals:
        copy.wait_recv()
    n_rows = 2 * HALF
    row = lax.broadcasted_iota(jnp.int32, (n_rows, HALF), 0)
    slot = lax.broadcasted_iota(jnp.int32, (n_rows, HALF), 1)
    start = jnp.zeros((1, HALF), jnp.int32)
    targets = jnp.zeros((n_rows, FB), F32)
    for q in range(NX):
        count = cnt_r[q, 0:1, :HALF]
        chosen = jnp.logical_and(row - start == slot, slot < count)
        targets += jnp.dot(chosen.astype(BF16), tea_r[q], preferred_element_type=F32)
        start = start + count
    ids_row = ids[...].astype(F32)
    row = lax.broadcasted_iota(jnp.int32, (n_rows, n_rows), 0)
    col = lax.broadcasted_iota(jnp.int32, (n_rows, n_rows), 1)
    diagonal = row == col
    ids_col = jnp.sum(jnp.where(diagonal, ids_row, 0.0), axis=1, keepdims=True)
    size = jnp.sum((ids_col == ids_row).astype(F32), axis=1, keepdims=True)
    weight = 1.0 / size

    final = jnp.concatenate(finals, axis=0)
    gain = fg[...]
    gained = final * gain
    columns = [
        jnp.sum(value, axis=1, keepdims=True)
        for value in (final * final, gained * gained, gained * targets, targets * targets)
    ]
    for i, column in enumerate(columns):
        sum_y[y, i:i + 1, :n_rows] = jnp.sum(jnp.where(diagonal, column, 0.0), axis=0, keepdims=True)
    sent = [link.put(sum_y.at[y], sum_y.at[y], peer_y(k)) for k in range(1, NY)]
    for copy in sent:
        copy.wait_recv()
    sum_z[z] = sum_y[0] + sum_y[1] + sum_y[2] + sum_y[3]
    sent = [link.put(sum_z.at[z], sum_z.at[z], peer_z(k)) for k in range(1, NZ)]
    for copy in sent:
        copy.wait_recv()
    sums = sum_z[0]
    for k in range(1, NZ):
        sums = sums + sum_z[k]
    s1, s2, s3, s4 = [
        jnp.sum(jnp.where(diagonal, sums[i:i + 1, :n_rows], 0.0), axis=1, keepdims=True) for i in range(4)
    ]
    rscale = lax.rsqrt(s1 / D + EPSILON)
    inner_sum = weight * (rscale * rscale * s2 - rscale * s3)
    errors = rscale * rscale * s2 - 2.0 * rscale * s3 + s4
    normal = final * rscale
    d_student = weight * (normal * gain - targets)
    out[...] = rscale * (gain * d_student - normal * (inner_sum / D))
    total = jnp.sum(weight * 0.5 * errors, axis=0, keepdims=True) / (DOCS * D)
    loss[...] = total

    link.finish()


def body(
    hidden_in, layer_gain, gate_proj, up_proj, down_proj, final_gain, teacher_rows, send_counts, doc_ids
):
    vmem = pl.BlockSpec(memory_space=pltpu.VMEM)
    smem = pl.BlockSpec(memory_space=pltpu.SMEM)
    hbm = pl.BlockSpec(memory_space=pl.ANY)
    scratch = [
        pltpu.VMEM((2, DB, 2 * FF_LOCAL), BF16),
        pltpu.VMEM((2, FF_LOCAL, DB), BF16),
        pltpu.VMEM((2, 1, DB), F32),
        pltpu.VMEM((2, 2, 2, NY, NX, HALF, FB), BF16),
        pltpu.VMEM((ROWS // 2, DB), BF16),
        pltpu.VMEM((2, 2, NX, HALF, PCOLS), BF16),
        pltpu.VMEM((2, 2, NX - 1, HALF, PCOLS), BF16),
        pltpu.VMEM((2, 2, NX, HALF, FF_LOCAL), BF16),
        pltpu.VMEM((2, 2, 2, NY, NX, HALF, FB), BF16),
        pltpu.VMEM((2, 2, NY - 1, 2, NX, HALF, FB), BF16),
        pltpu.VMEM((2, NZ - 1, HALF, FB), BF16),
        pltpu.VMEM((2, HALF, FB), BF16),
        pltpu.VMEM((2, NZ, HALF, FB), BF16),
        pltpu.VMEM((NX, HALF, FB), BF16),
        pltpu.VMEM((NX, 8, 128), jnp.int32),
        pltpu.VMEM((NX, 8, 128), jnp.int32),
        pltpu.VMEM((NY, 8, 128), F32),
        pltpu.VMEM((NZ, 8, 128), F32),
        pltpu.SemaphoreType.DMA((N_SEMS,)),
        pltpu.SemaphoreType.DMA((N_SEMS,)),
    ]
    grad, loss = pl.pallas_call(
        kernel,
        out_shape=(
            jax.ShapeDtypeStruct((2 * HALF, FB), F32),
            jax.ShapeDtypeStruct((1, 1), F32),
        ),
        in_specs=[vmem, vmem, smem, vmem, vmem, hbm, hbm, hbm, hbm],
        out_specs=(vmem, vmem),
        scratch_shapes=scratch,
        compiler_params=pltpu.CompilerParams(
            collective_id=0, has_side_effects=True, vmem_limit_bytes=56 * 1024 * 1024
        ),
    )(
        hidden_in.reshape(2, HALF, FB),
        teacher_rows.reshape(NX, HALF, FB),
        send_counts.reshape(1, NX),
        doc_ids.reshape(1, 2 * HALF),
        final_gain.reshape(1, FB),
        layer_gain,
        gate_proj,
        up_proj,
        down_proj,
    )
    return grad[None], loss


def solution(mesh):
    in_specs = (
        P("section", "dp", "mp"),
        P(None, "section", None),
        P(None, "section", "dp", "mp"),
        P(None, "section", "dp", "mp"),
        P(None, "section", "mp", "dp"),
        P("mp"),
        P("section", "dp", None, "mp"),
        P("section", "dp", None),
        P("section", "dp", None),
    )
    out_specs = (P("section", "dp", "mp"), P("section", "dp"))
    return jax.shard_map(body, mesh=mesh, in_specs=in_specs, out_specs=out_specs, check_vma=False)
```

```python
import functools

import jax
import jax.numpy as jnp
from jax import lax
from jax.experimental import pallas as pl
from jax.experimental.pallas import tpu as pltpu
from jax.sharding import PartitionSpec as P

D = 8192
DOCS = 8
EPSILON = 1e-05
NX, NY, NZ = 4, 4, 8
CHUNKS = 3
HALF = 96 // CHUNKS
ROWS = NX * HALF
CAP = 48
FB = 256
FF_LOCAL = 512
DB = 2048
EXTRA = 128
PCOLS = 2 * FF_LOCAL + EXTRA
N_SEMS = 256
MESH = pl.DeviceIdType.MESH
ORDER = "0010210121202102103210201012102212102"
LAG = 6
F32 = jnp.float32
BF16 = jnp.bfloat16


class Link:
    def __init__(self, send_sems, recv_sems):
        self.send_sems, self.recv_sems = send_sems, recv_sems
        self.used = 0
        self.sent = []
        self.drained = 0

    def take(self, count=1):
        first = self.used
        self.used += count
        return first

    def make(self, src, dst, peer, send, recv):
        return pltpu.make_async_remote_copy(
            src_ref=src,
            dst_ref=dst,
            send_sem=self.send_sems.at[send],
            recv_sem=self.recv_sems.at[recv],
            device_id=peer,
            device_id_type=MESH,
        )

    def put(self, src, dst, peer):
        i = self.take()
        copy = self.make(src, dst, peer, i, i)
        copy.start()
        self.sent.append((None, copy))
        return copy

    def put_if(self, needed, src, dst, peer, send, recv):
        copy = self.make(src, dst, peer, send, recv)
        pl.when(needed)(lambda: copy.start())
        self.sent.append((needed, copy))

    def local(self, src, dst):
        copy = pltpu.make_async_copy(src, dst, self.recv_sems.at[self.take()])
        copy.start()
        return copy

    def drain(self, upto):
        while self.drained < upto:
            needed, copy = self.sent[self.drained]
            self.drained += 1
            if needed is None:
                copy.wait_send()
            else:
                pl.when(needed)(lambda copy=copy: copy.wait_send())


def drive(order, gens, link):
    marks = []
    for name in order:
        if len(marks) > LAG:
            link.drain(marks[-1 - LAG])
        next(gens[int(name)], None)
        marks.append(len(link.sent))
    for gen in gens:
        assert next(gen, "end") == "end"


def kernel(
    hid, tea, cnt, ids, fg, lg, gate, up, down,
    out, loss,
    w1, w2, gains, xs, xn, parts, part_r, inn, terms,
    y_r, z_r, kept, last_r,
    tea_r, cnt_s, cnt_r, targets, weights, final, sum_y, sum_z,
    send_sems, recv_sems,
):
    s = lax.axis_index("section")
    x = lax.axis_index("dp")
    m = lax.axis_index("mp")
    y, z = lax.rem(m, NY), lax.div(m, NY)
    a, b = lax.div(z, 2), lax.rem(z, 2)
    o = 1 - s
    link = Link(send_sems, recv_sems)

    def at_y(k):
        return lax.rem(y + k + NY, NY)

    def at_z(k):
        return lax.rem(z + k + NZ, NZ)

    def at_x(k):
        return lax.rem(x + k + NX, NX)

    def peer_y(k):
        return {"mp": z * NY + at_y(k)}

    def peer_z(k):
        return {"mp": at_z(k) * NY + y}

    def peer_x(k):
        return {"dp": at_x(k)}

    core = {"section": o}
    swap = {"dp": a, "mp": (2 * x + b) * NY + y}
    own_side = a == x
    planes = [{"dp": a, "mp": j * NY + y} for j in range(NZ)]
    homes = [{"dp": j // 2, "mp": (2 * x + j % 2) * NY + y} for j in range(NZ)]

    def other(j):
        return jnp.logical_not(jnp.logical_and(own_side, z == j))

    barrier = pltpu.get_barrier_semaphore()
    peers = (
        [peer_y(k) for k in range(1, NY)]
        + [peer_z(k) for k in range(1, NZ)]
        + [peer_x(k) for k in range(1, NX)]
        + [core]
    )
    for group in (homes, planes):
        for j, peer in enumerate(group):

            @pl.when(other(j))
            def _():
                pl.semaphore_signal(barrier, inc=1, device_id=peer, device_id_type=MESH)

    for peer in peers:
        pl.semaphore_signal(barrier, inc=1, device_id=peer, device_id_type=MESH)

    loads = [
        link.local(gate.at[0, 0], w1.at[s, :, pl.ds(0, FF_LOCAL)]),
        link.local(up.at[0, 0], w1.at[s, :, pl.ds(FF_LOCAL, FF_LOCAL)]),
        link.local(down.at[0, 0], w2.at[s]),
        link.local(lg.at[0, :, pl.ds(pl.multiple_of(x * DB, DB), DB)], gains.at[s]),
    ]
    many = len(peers) + 2 * NZ
    pl.semaphore_wait(barrier, jnp.where(own_side, many - 2, many))

    def spread(group, src, dst, key):
        first = link.take(NZ)
        for j in range(NZ):
            link.put_if(other(j), src(j), dst, group[j], first + j, first + key)
        return first

    def collect(first, ref):
        for j in range(NZ):
            copy = link.make(ref, ref, swap, first + j, first + j)
            pl.when(other(j))(lambda copy=copy: copy.wait_recv())


    def order(n):
        return sorted(range(1, n), key=lambda k: -min(k, n - k))

    def gather_direct(block, pos, peer, n):
        mine = block(pos(0))
        copies = [link.put(mine, mine, peer(k)) for k in order(n)]
        yield
        for copy in copies:
            copy.wait_recv()

    def scatter_direct(block, pos, peer, n, slot, finish):
        copies = [link.put(block(pos(k)), slot(k - 1), peer(k)) for k in order(n)]
        yield
        for copy in copies:
            copy.wait_recv()
        finish(block(pos(0)), [slot(k - 1) for k in range(1, n)])


    def widen(l, c):
        squares = jnp.zeros((ROWS, 128), F32)
        for k in range(8):
            kb, ky = divmod(k, NY)
            value = xs[l, c, kb, ky].reshape(ROWS, FB).astype(F32)
            xn[:, k * FB:(k + 1) * FB] = (value * gains[l, :, k * FB:(k + 1) * FB]).astype(BF16)
            square = value * value
            squares = squares + square[:, :128] + square[:, 128:]
        return jnp.sum(squares, axis=-1, keepdims=True)

    def split_sum(total):
        wide = jnp.broadcast_to(total, total.shape[:-1] + (EXTRA,))
        head = wide.astype(BF16).astype(F32)
        lane = lax.broadcasted_iota(jnp.int32, wide.shape, wide.ndim - 1)
        return jnp.where(lane < EXTRA // 2, head, wide - head).astype(BF16)

    def join_sum(tile):
        return jnp.sum(tile.astype(F32), axis=-1, keepdims=True) * (2.0 / EXTRA)

    def gate_up(l, c):
        extra = split_sum(widen(l, c)).reshape(NX, HALF, EXTRA)
        parts[l, c, :, :, 2 * FF_LOCAL:] = extra
        for n in range(4):
            value = jnp.dot(xn[...], w1[l, :, n * FB:(n + 1) * FB], preferred_element_type=F32)
            parts[l, c, :, :, n * FB:(n + 1) * FB] = value.astype(BF16).reshape(NX, HALF, FB)

    def reduce_parts(l, c):
        def finish(mine, others):
            every = [mine] + others
            squares = sum(join_sum(ref[:, 2 * FF_LOCAL:]) for ref in every)
            scale = lax.rsqrt(squares / D + EPSILON)

            def total(first):
                return sum(ref[:, first:first + FF_LOCAL].astype(F32) for ref in every) * scale

            act = total(0)
            inn[l, c, x] = (act / (1.0 + jnp.exp(-act)) * total(FF_LOCAL)).astype(BF16)

        yield from scatter_direct(
            lambda q: parts.at[l, c, q], at_x, peer_x, NX, lambda i: part_r.at[l, c, i], finish
        )

    def down_terms(l, c):
        rows = inn[l, c].reshape(ROWS, FF_LOCAL)
        for n in range(8):
            nb, ny = divmod(n, NY)
            value = jnp.dot(rows, w2[l, :, n * FB:(n + 1) * FB], preferred_element_type=F32)
            terms[l, c, nb, ny] = value.astype(BF16).reshape(NX, HALF, FB)

    def add_up(mine, others):
        return sum((ref[...].astype(F32) for ref in others), mine[...].astype(F32))

    def sum_terms(mine, others):
        mine[...] = add_up(mine, others).astype(BF16)

    def chain(c):
        landing = xs.at[0, c, b, y, x]
        first = spread(planes, lambda j: hid.at[c], landing, 2 * x + b)

        here = pltpu.make_async_copy(hid.at[c], landing, recv_sems.at[link.take()])
        pl.when(own_side)(lambda: here.start())
        yield
        pl.when(own_side)(lambda: here.wait())
        collect(first, landing)
        for l in range(2):
            if l == 1:
                yield from gather_direct(
                    lambda q: xs.at[1, c, lax.rem(q, 2), y, lax.div(q, 2)], at_z, peer_z, NZ
                )
            yield from gather_direct(lambda q: xs.at[l, c, :, q], at_y, peer_y, NY)
            if l == 0 and c == 0:
                for copy in loads:
                    copy.wait()
                for copy in crossing:
                    copy.wait_recv()
            gate_up(l, c)
            yield from reduce_parts(l, c)
            yield from gather_direct(lambda q: inn.at[l, c, q], at_x, peer_x, NX)
            down_terms(l, c)
            yield from scatter_direct(
                lambda q: terms.at[l, c, :, q], at_y, peer_y, NY, lambda i: y_r.at[l, c, i], sum_terms
            )
            if l == 0:
                def finish(mine, others):
                    fresh = xs[0, c, b, y, a].astype(F32) + add_up(mine, others)
                    xs[1, c, b, y, a] = fresh.astype(BF16)

                yield from scatter_direct(
                    lambda q: terms.at[0, c, lax.rem(q, 2), y, lax.div(q, 2)],
                    at_z, peer_z, NZ, lambda i: z_r.at[c, i], finish,
                )
                base = link.take()
                link.put_if(
                    jnp.logical_not(own_side), xs.at[1, c, b, y, a], kept.at[c], swap, base, base
                )
                state_sems[c] = base

                @pl.when(own_side)
                def _():
                    kept[c] = xs[1, c, b, y, a]

        first = spread(homes, lambda j: terms.at[1, c, j % 2, y, j // 2], last_r.at[c, z], z)

        @pl.when(own_side)
        def _():
            last_r[c, z] = terms[1, c, b, y, a]

        yield
        collect(first, last_r.at[c, 0])
        copy = link.make(kept.at[c], kept.at[c], swap, state_sems[c], state_sems[c])
        pl.when(jnp.logical_not(own_side))(lambda: copy.wait_recv())
        value = kept[c].astype(F32)
        for j in range(NZ):
            value = value + last_r[c, j].astype(F32)
        value = value.astype(BF16).astype(F32)
        final[c * HALF:(c + 1) * HALF] = value
        gained = value * fg[...]
        wanted = targets[c * HALF:(c + 1) * HALF]
        for i, product in enumerate((value * value, gained * gained, gained * wanted, wanted * wanted)):
            sums_of[i].append(as_row(jnp.sum(product, axis=1, keepdims=True), c * HALF))

    n_rows = CHUNKS * HALF
    state_sems, sums_of = [None] * CHUNKS, [[] for _ in range(4)]
    diagonal = lax.broadcasted_iota(jnp.int32, (n_rows, n_rows), 0) == lax.broadcasted_iota(
        jnp.int32, (n_rows, n_rows), 1
    )

    def as_row(column, first):
        shape = (column.shape[0], n_rows)
        own = lax.broadcasted_iota(jnp.int32, shape, 0) + first == lax.broadcasted_iota(jnp.int32, shape, 1)
        return jnp.sum(jnp.where(own, column, 0.0), axis=0, keepdims=True)

    def as_column(line):
        return jnp.sum(jnp.where(diagonal, line, 0.0), axis=1, keepdims=True)

    def prepare():
        own_rows.wait()
        for copy in arrivals:
            copy.wait_recv()
        row = lax.broadcasted_iota(jnp.int32, (n_rows, CAP), 0)
        slot = lax.broadcasted_iota(jnp.int32, (n_rows, CAP), 1)
        start = jnp.zeros((1, CAP), jnp.int32)
        value = jnp.zeros((n_rows, FB), F32)
        for q in range(NX):
            count = cnt_r[q, 0:1, :CAP]
            chosen = jnp.logical_and(row - start == slot, slot < count)
            value += jnp.dot(chosen.astype(BF16), tea_r[q], preferred_element_type=F32)
            start = start + count
        targets[...] = value
        ids_row = ids[...].astype(F32)
        size = jnp.sum((as_column(ids_row) == ids_row).astype(F32), axis=1, keepdims=True)
        weights[...] = jnp.broadcast_to(1.0 / size, weights.shape)
        yield


    chains = [chain(c) for c in range(CHUNKS)]
    for gen in chains:
        next(gen)

    gain_block = lg.at[0, :, pl.ds(pl.multiple_of(x * DB, DB), DB)]
    crossing = [
        link.put(gain_block, gains.at[s], core),
        link.put(gate.at[0, 0], w1.at[s, :, pl.ds(0, FF_LOCAL)], core),
        link.put(up.at[0, 0], w1.at[s, :, pl.ds(FF_LOCAL, FF_LOCAL)], core),
        link.put(down.at[0, 0], w2.at[s], core),
    ]

    for p in range(NX):
        cnt_s[p] = jnp.full((8, 128), cnt[0, p], jnp.int32)
    arrivals = []
    for k in range(1, NX):
        arrivals.append(link.put(tea.at[at_x(k)], tea_r.at[x], peer_x(k)))
        arrivals.append(link.put(cnt_s.at[at_x(k)], cnt_r.at[x], peer_x(k)))
    own_rows = link.local(tea.at[x], tea_r.at[x])
    cnt_r[x] = cnt_s[x]

    drive(ORDER, chains + [prepare()], link)

    for i, lines in enumerate(sums_of):
        sum_y[y, i:i + 1, :n_rows] = sum(lines)
    before = len(link.sent)
    sent = [link.put(sum_y.at[y], sum_y.at[y], peer_y(k)) for k in range(1, NY)]
    link.drain(before)
    for copy in sent:
        copy.wait_recv()
    sum_z[z] = sum_y[0] + sum_y[1] + sum_y[2] + sum_y[3]
    sent = [link.put(sum_z.at[z], sum_z.at[z], peer_z(k)) for k in range(1, NZ)]
    for copy in sent:
        copy.wait_recv()
    sums = sum_z[0]
    for k in range(1, NZ):
        sums = sums + sum_z[k]
    s1, s2, s3, s4 = [as_column(sums[i:i + 1, :n_rows]) for i in range(4)]
    weight = weights[:, :1]
    gain = fg[...]
    rscale = lax.rsqrt(s1 / D + EPSILON)
    inner_sum = weight * (rscale * rscale * s2 - rscale * s3)
    errors = rscale * rscale * s2 - 2.0 * rscale * s3 + s4
    normal = final[...] * rscale
    d_student = weight * (normal * gain - targets[...])
    out[...] = rscale * (gain * d_student - normal * (inner_sum / D))
    total = jnp.sum(weight * 0.5 * errors, axis=0, keepdims=True) / (DOCS * D)
    loss[...] = total

    link.drain(len(link.sent))


def body(
    hidden_in, layer_gain, gate_proj, up_proj, down_proj, final_gain, teacher_rows, send_counts, doc_ids
):
    vmem = pl.BlockSpec(memory_space=pltpu.VMEM)
    smem = pl.BlockSpec(memory_space=pltpu.SMEM)
    hbm = pl.BlockSpec(memory_space=pl.ANY)
    scratch = [
        pltpu.VMEM((2, DB, 2 * FF_LOCAL), BF16),
        pltpu.VMEM((2, FF_LOCAL, DB), BF16),
        pltpu.VMEM((2, 1, DB), F32),
        pltpu.VMEM((2, CHUNKS, 2, NY, NX, HALF, FB), BF16),
        pltpu.VMEM((ROWS, DB), BF16),
        pltpu.VMEM((2, CHUNKS, NX, HALF, PCOLS), BF16),
        pltpu.VMEM((2, CHUNKS, NX - 1, HALF, PCOLS), BF16),
        pltpu.VMEM((2, CHUNKS, NX, HALF, FF_LOCAL), BF16),
        pltpu.VMEM((2, CHUNKS, 2, NY, NX, HALF, FB), BF16),
        pltpu.VMEM((2, CHUNKS, NY - 1, 2, NX, HALF, FB), BF16),
        pltpu.VMEM((CHUNKS, NZ - 1, HALF, FB), BF16),
        pltpu.VMEM((CHUNKS, HALF, FB), BF16),
        pltpu.VMEM((CHUNKS, NZ, HALF, FB), BF16),
        pltpu.VMEM((NX, CAP, FB), BF16),
        pltpu.VMEM((NX, 8, 128), jnp.int32),
        pltpu.VMEM((NX, 8, 128), jnp.int32),
        pltpu.VMEM((CHUNKS * HALF, FB), F32),
        pltpu.VMEM((CHUNKS * HALF, 128), F32),
        pltpu.VMEM((CHUNKS * HALF, FB), F32),
        pltpu.VMEM((NY, 8, 128), F32),
        pltpu.VMEM((NZ, 8, 128), F32),
        pltpu.SemaphoreType.DMA((N_SEMS,)),
        pltpu.SemaphoreType.DMA((N_SEMS,)),
    ]
    grad, loss = pl.pallas_call(
        kernel,
        out_shape=(
            jax.ShapeDtypeStruct((CHUNKS * HALF, FB), F32),
            jax.ShapeDtypeStruct((1, 1), F32),
        ),
        in_specs=[hbm, hbm, smem, vmem, vmem, hbm, hbm, hbm, hbm],
        out_specs=(vmem, vmem),
        scratch_shapes=scratch,
        compiler_params=pltpu.CompilerParams(
            collective_id=0, has_side_effects=True, vmem_limit_bytes=56 * 1024 * 1024
        ),
    )(
        hidden_in.reshape(CHUNKS, HALF, FB),
        teacher_rows.reshape(NX, CAP, FB),
        send_counts.reshape(1, NX),
        doc_ids.reshape(1, CHUNKS * HALF),
        final_gain.reshape(1, FB),
        layer_gain,
        gate_proj,
        up_proj,
        down_proj,
    )
    return grad[None], loss


def solution(mesh):
    in_specs = (
        P("section", "dp", "mp"),
        P(None, "section", None),
        P(None, "section", "dp", "mp"),
        P(None, "section", "dp", "mp"),
        P(None, "section", "mp", "dp"),
        P("mp"),
        P("section", "dp", None, "mp"),
        P("section", "dp", None),
        P("section", "dp", None),
    )
    out_specs = (P("section", "dp", "mp"), P("section", "dp"))
    return jax.shard_map(body, mesh=mesh, in_specs=in_specs, out_specs=out_specs, check_vma=False)
```

```python
import functools

import jax
import jax.numpy as jnp
from jax import lax
from jax.experimental import pallas as pl
from jax.experimental.pallas import tpu as pltpu
from jax.sharding import PartitionSpec as P

D = 8192
DOCS = 8
EPSILON = 1e-05
NX, NY, NZ = 4, 4, 8
CHUNKS = 6
HALF = 96 // CHUNKS
ROWS = NX * HALF
CAP = 48
FB = 256
FF_LOCAL = 512
DB = 2048
EXTRA = 128
PCOLS = 2 * FF_LOCAL + EXTRA
N_SEMS = 400
MESH = pl.DeviceIdType.MESH
ORDER = "0120314023512043152045314250312043516243051420512041352430415325403532145"
LAG = 12
F32 = jnp.float32
BF16 = jnp.bfloat16


class Link:
    def __init__(self, send_sems, recv_sems):
        self.send_sems, self.recv_sems = send_sems, recv_sems
        self.used = 0
        self.sent = []
        self.drained = 0

    def take(self, count=1):
        first = self.used
        self.used += count
        return first

    def make(self, src, dst, peer, send, recv):
        return pltpu.make_async_remote_copy(
            src_ref=src,
            dst_ref=dst,
            send_sem=self.send_sems.at[send],
            recv_sem=self.recv_sems.at[recv],
            device_id=peer,
            device_id_type=MESH,
        )

    def put(self, src, dst, peer):
        i = self.take()
        copy = self.make(src, dst, peer, i, i)
        copy.start()
        self.sent.append((None, copy))
        return copy

    def put_if(self, needed, src, dst, peer, send, recv):
        copy = self.make(src, dst, peer, send, recv)
        pl.when(needed)(lambda: copy.start())
        self.sent.append((needed, copy))

    def local(self, src, dst):
        copy = pltpu.make_async_copy(src, dst, self.recv_sems.at[self.take()])
        copy.start()
        return copy

    def drain(self, upto):
        while self.drained < upto:
            needed, copy = self.sent[self.drained]
            self.drained += 1
            if needed is None:
                copy.wait_send()
            else:
                pl.when(needed)(lambda copy=copy: copy.wait_send())


def drive(order, gens, link):
    marks = []
    for name in order:
        if len(marks) > LAG:
            link.drain(marks[-1 - LAG])
        next(gens[int(name)], None)
        marks.append(len(link.sent))
    for gen in gens:
        assert next(gen, "end") == "end"


def kernel(
    hid, tea, cnt, ids, fg, lg, gate, up, down,
    out, loss,
    w1, w2, gains, xs, xn, parts, part_r, inn, terms,
    y_r, z_r, kept, last_r,
    tea_r, cnt_s, cnt_r, targets, weights, final, sum_y, sum_z,
    send_sems, recv_sems,
):
    s = lax.axis_index("section")
    x = lax.axis_index("dp")
    m = lax.axis_index("mp")
    y, z = lax.rem(m, NY), lax.div(m, NY)
    a, b = lax.div(z, 2), lax.rem(z, 2)
    o = 1 - s
    link = Link(send_sems, recv_sems)

    def at_y(k):
        return lax.rem(y + k + NY, NY)

    def at_z(k):
        return lax.rem(z + k + NZ, NZ)

    def at_x(k):
        return lax.rem(x + k + NX, NX)

    def peer_y(k):
        return {"mp": z * NY + at_y(k)}

    def peer_z(k):
        return {"mp": at_z(k) * NY + y}

    def peer_x(k):
        return {"dp": at_x(k)}

    core = {"section": o}
    swap = {"dp": a, "mp": (2 * x + b) * NY + y}
    own_side = a == x
    planes = [{"dp": a, "mp": j * NY + y} for j in range(NZ)]
    homes = [{"dp": j // 2, "mp": (2 * x + j % 2) * NY + y} for j in range(NZ)]

    def other(j):
        return jnp.logical_not(jnp.logical_and(own_side, z == j))

    barrier = pltpu.get_barrier_semaphore()
    peers = (
        [peer_y(k) for k in range(1, NY)]
        + [peer_z(k) for k in range(1, NZ)]
        + [peer_x(k) for k in range(1, NX)]
        + [core]
    )
    for group in (homes, planes):
        for j, peer in enumerate(group):

            @pl.when(other(j))
            def _():
                pl.semaphore_signal(barrier, inc=1, device_id=peer, device_id_type=MESH)

    for peer in peers:
        pl.semaphore_signal(barrier, inc=1, device_id=peer, device_id_type=MESH)

    loads = [
        link.local(gate.at[0, 0], w1.at[s, :, pl.ds(0, FF_LOCAL)]),
        link.local(up.at[0, 0], w1.at[s, :, pl.ds(FF_LOCAL, FF_LOCAL)]),
        link.local(down.at[0, 0], w2.at[s]),
        link.local(lg.at[0, :, pl.ds(pl.multiple_of(x * DB, DB), DB)], gains.at[s]),
    ]
    many = len(peers) + 2 * NZ
    pl.semaphore_wait(barrier, jnp.where(own_side, many - 2, many))

    def spread(group, src, dst, key):
        first = link.take(NZ)
        for j in range(NZ):
            link.put_if(other(j), src(j), dst, group[j], first + j, first + key)
        return first

    def collect(first, ref):
        for j in range(NZ):
            copy = link.make(ref, ref, swap, first + j, first + j)
            pl.when(other(j))(lambda copy=copy: copy.wait_recv())


    def order(n):
        return sorted(range(1, n), key=lambda k: -min(k, n - k))

    def gather_direct(block, pos, peer, n):
        mine = block(pos(0))
        copies = [link.put(mine, mine, peer(k)) for k in order(n)]
        yield
        for copy in copies:
            copy.wait_recv()

    def scatter_direct(block, pos, peer, n, slot, finish):
        copies = [link.put(block(pos(k)), slot(k - 1), peer(k)) for k in order(n)]
        yield
        for copy in copies:
            copy.wait_recv()
        finish(block(pos(0)), [slot(k - 1) for k in range(1, n)])


    def widen(l, c):
        squares = jnp.zeros((ROWS, 128), F32)
        for k in range(8):
            kb, ky = divmod(k, NY)
            value = xs[l, c, kb, ky].reshape(ROWS, FB).astype(F32)
            xn[:, k * FB:(k + 1) * FB] = (value * gains[l, :, k * FB:(k + 1) * FB]).astype(BF16)
            square = value * value
            squares = squares + square[:, :128] + square[:, 128:]
        return jnp.sum(squares, axis=-1, keepdims=True)

    def split_sum(total):
        wide = jnp.broadcast_to(total, total.shape[:-1] + (EXTRA,))
        head = wide.astype(BF16).astype(F32)
        lane = lax.broadcasted_iota(jnp.int32, wide.shape, wide.ndim - 1)
        return jnp.where(lane < EXTRA // 2, head, wide - head).astype(BF16)

    def join_sum(tile):
        return jnp.sum(tile.astype(F32), axis=-1, keepdims=True) * (2.0 / EXTRA)

    def gate_up(l, c):
        extra = split_sum(widen(l, c)).reshape(NX, HALF, EXTRA)
        parts[l, c, :, :, 2 * FF_LOCAL:] = extra
        for n in range(4):
            value = jnp.dot(xn[...], w1[l, :, n * FB:(n + 1) * FB], preferred_element_type=F32)
            parts[l, c, :, :, n * FB:(n + 1) * FB] = value.astype(BF16).reshape(NX, HALF, FB)

    def reduce_parts(l, c):
        def finish(mine, others):
            every = [mine] + others
            squares = sum(join_sum(ref[:, 2 * FF_LOCAL:]) for ref in every)
            scale = lax.rsqrt(squares / D + EPSILON)

            def total(first):
                return sum(ref[:, first:first + FF_LOCAL].astype(F32) for ref in every) * scale

            act = total(0)
            inn[l, c, x] = (act / (1.0 + jnp.exp(-act)) * total(FF_LOCAL)).astype(BF16)

        yield from scatter_direct(
            lambda q: parts.at[l, c, q], at_x, peer_x, NX, lambda i: part_r.at[l, c, i], finish
        )

    def down_terms(l, c):
        rows = inn[l, c].reshape(ROWS, FF_LOCAL)
        for n in range(8):
            nb, ny = divmod(n, NY)
            value = jnp.dot(rows, w2[l, :, n * FB:(n + 1) * FB], preferred_element_type=F32)
            terms[l, c, nb, ny] = value.astype(BF16).reshape(NX, HALF, FB)

    def add_up(mine, others):
        return sum((ref[...].astype(F32) for ref in others), mine[...].astype(F32))

    def sum_terms(mine, others):
        mine[...] = add_up(mine, others).astype(BF16)

    def chain(c):
        landing = xs.at[0, c, b, y, x]
        first = spread(planes, lambda j: hid.at[c], landing, 2 * x + b)

        here = pltpu.make_async_copy(hid.at[c], landing, recv_sems.at[link.take()])
        pl.when(own_side)(lambda: here.start())
        yield
        pl.when(own_side)(lambda: here.wait())
        collect(first, landing)
        for l in range(2):
            if l == 1:
                yield from gather_direct(
                    lambda q: xs.at[1, c, lax.rem(q, 2), y, lax.div(q, 2)], at_z, peer_z, NZ
                )
            yield from gather_direct(lambda q: xs.at[l, c, :, q], at_y, peer_y, NY)
            if l == 0 and c == 0:
                for copy in loads:
                    copy.wait()
                for copy in crossing:
                    copy.wait_recv()
            gate_up(l, c)
            yield from reduce_parts(l, c)
            yield from gather_direct(lambda q: inn.at[l, c, q], at_x, peer_x, NX)
            down_terms(l, c)
            yield from scatter_direct(
                lambda q: terms.at[l, c, :, q], at_y, peer_y, NY, lambda i: y_r.at[l, c, i], sum_terms
            )
            if l == 0:
                def finish(mine, others):
                    fresh = xs[0, c, b, y, a].astype(F32) + add_up(mine, others)
                    xs[1, c, b, y, a] = fresh.astype(BF16)

                yield from scatter_direct(
                    lambda q: terms.at[0, c, lax.rem(q, 2), y, lax.div(q, 2)],
                    at_z, peer_z, NZ, lambda i: z_r.at[c, i], finish,
                )
                base = link.take()
                link.put_if(
                    jnp.logical_not(own_side), xs.at[1, c, b, y, a], kept.at[c], swap, base, base
                )
                state_sems[c] = base

                @pl.when(own_side)
                def _():
                    kept[c] = xs[1, c, b, y, a]

        first = spread(homes, lambda j: terms.at[1, c, j % 2, y, j // 2], last_r.at[c, z], z)

        @pl.when(own_side)
        def _():
            last_r[c, z] = terms[1, c, b, y, a]

        yield
        collect(first, last_r.at[c, 0])
        copy = link.make(kept.at[c], kept.at[c], swap, state_sems[c], state_sems[c])
        pl.when(jnp.logical_not(own_side))(lambda: copy.wait_recv())
        value = kept[c].astype(F32)
        for j in range(NZ):
            value = value + last_r[c, j].astype(F32)
        value = value.astype(BF16).astype(F32)
        final[c * HALF:(c + 1) * HALF] = value
        gained = value * fg[...]
        wanted = targets[c * HALF:(c + 1) * HALF]
        for i, product in enumerate((value * value, gained * gained, gained * wanted, wanted * wanted)):
            sums_of[i].append(as_row(jnp.sum(product, axis=1, keepdims=True), c * HALF))

    n_rows = CHUNKS * HALF
    state_sems, sums_of = [None] * CHUNKS, [[] for _ in range(4)]
    diagonal = lax.broadcasted_iota(jnp.int32, (n_rows, n_rows), 0) == lax.broadcasted_iota(
        jnp.int32, (n_rows, n_rows), 1
    )

    def as_row(column, first):
        shape = (column.shape[0], n_rows)
        own = lax.broadcasted_iota(jnp.int32, shape, 0) + first == lax.broadcasted_iota(jnp.int32, shape, 1)
        return jnp.sum(jnp.where(own, column, 0.0), axis=0, keepdims=True)

    def as_column(line):
        return jnp.sum(jnp.where(diagonal, line, 0.0), axis=1, keepdims=True)

    def prepare():
        own_rows.wait()
        for copy in arrivals:
            copy.wait_recv()
        row = lax.broadcasted_iota(jnp.int32, (n_rows, CAP), 0)
        slot = lax.broadcasted_iota(jnp.int32, (n_rows, CAP), 1)
        start = jnp.zeros((1, CAP), jnp.int32)
        value = jnp.zeros((n_rows, FB), F32)
        for q in range(NX):
            count = cnt_r[q, 0:1, :CAP]
            chosen = jnp.logical_and(row - start == slot, slot < count)
            value += jnp.dot(chosen.astype(BF16), tea_r[q], preferred_element_type=F32)
            start = start + count
        targets[...] = value
        ids_row = ids[...].astype(F32)
        size = jnp.sum((as_column(ids_row) == ids_row).astype(F32), axis=1, keepdims=True)
        weights[...] = jnp.broadcast_to(1.0 / size, weights.shape)
        yield


    chains = [chain(c) for c in range(CHUNKS)]
    for gen in chains:
        next(gen)

    gain_block = lg.at[0, :, pl.ds(pl.multiple_of(x * DB, DB), DB)]
    crossing = [
        link.put(gain_block, gains.at[s], core),
        link.put(gate.at[0, 0], w1.at[s, :, pl.ds(0, FF_LOCAL)], core),
        link.put(up.at[0, 0], w1.at[s, :, pl.ds(FF_LOCAL, FF_LOCAL)], core),
        link.put(down.at[0, 0], w2.at[s], core),
    ]

    for p in range(NX):
        cnt_s[p] = jnp.full((8, 128), cnt[0, p], jnp.int32)
    arrivals = []
    for k in range(1, NX):
        arrivals.append(link.put(tea.at[at_x(k)], tea_r.at[x], peer_x(k)))
        arrivals.append(link.put(cnt_s.at[at_x(k)], cnt_r.at[x], peer_x(k)))
    own_rows = link.local(tea.at[x], tea_r.at[x])
    cnt_r[x] = cnt_s[x]

    drive(ORDER, chains + [prepare()], link)

    for i, lines in enumerate(sums_of):
        sum_y[y, i:i + 1, :n_rows] = sum(lines)
    before = len(link.sent)
    sent = [link.put(sum_y.at[y], sum_y.at[y], peer_y(k)) for k in range(1, NY)]
    link.drain(before)
    for copy in sent:
        copy.wait_recv()
    sum_z[z] = sum_y[0] + sum_y[1] + sum_y[2] + sum_y[3]
    sent = [link.put(sum_z.at[z], sum_z.at[z], peer_z(k)) for k in range(1, NZ)]
    for copy in sent:
        copy.wait_recv()
    sums = sum_z[0]
    for k in range(1, NZ):
        sums = sums + sum_z[k]
    s1, s2, s3, s4 = [as_column(sums[i:i + 1, :n_rows]) for i in range(4)]
    weight = weights[:, :1]
    gain = fg[...]
    rscale = lax.rsqrt(s1 / D + EPSILON)
    inner_sum = weight * (rscale * rscale * s2 - rscale * s3)
    errors = rscale * rscale * s2 - 2.0 * rscale * s3 + s4
    normal = final[...] * rscale
    d_student = weight * (normal * gain - targets[...])
    out[...] = rscale * (gain * d_student - normal * (inner_sum / D))
    total = jnp.sum(weight * 0.5 * errors, axis=0, keepdims=True) / (DOCS * D)
    loss[...] = total

    link.drain(len(link.sent))


def body(
    hidden_in, layer_gain, gate_proj, up_proj, down_proj, final_gain, teacher_rows, send_counts, doc_ids
):
    vmem = pl.BlockSpec(memory_space=pltpu.VMEM)
    smem = pl.BlockSpec(memory_space=pltpu.SMEM)
    hbm = pl.BlockSpec(memory_space=pl.ANY)
    scratch = [
        pltpu.VMEM((2, DB, 2 * FF_LOCAL), BF16),
        pltpu.VMEM((2, FF_LOCAL, DB), BF16),
        pltpu.VMEM((2, 1, DB), F32),
        pltpu.VMEM((2, CHUNKS, 2, NY, NX, HALF, FB), BF16),
        pltpu.VMEM((ROWS, DB), BF16),
        pltpu.VMEM((2, CHUNKS, NX, HALF, PCOLS), BF16),
        pltpu.VMEM((2, CHUNKS, NX - 1, HALF, PCOLS), BF16),
        pltpu.VMEM((2, CHUNKS, NX, HALF, FF_LOCAL), BF16),
        pltpu.VMEM((2, CHUNKS, 2, NY, NX, HALF, FB), BF16),
        pltpu.VMEM((2, CHUNKS, NY - 1, 2, NX, HALF, FB), BF16),
        pltpu.VMEM((CHUNKS, NZ - 1, HALF, FB), BF16),
        pltpu.VMEM((CHUNKS, HALF, FB), BF16),
        pltpu.VMEM((CHUNKS, NZ, HALF, FB), BF16),
        pltpu.VMEM((NX, CAP, FB), BF16),
        pltpu.VMEM((NX, 8, 128), jnp.int32),
        pltpu.VMEM((NX, 8, 128), jnp.int32),
        pltpu.VMEM((CHUNKS * HALF, FB), F32),
        pltpu.VMEM((CHUNKS * HALF, 128), F32),
        pltpu.VMEM((CHUNKS * HALF, FB), F32),
        pltpu.VMEM((NY, 8, 128), F32),
        pltpu.VMEM((NZ, 8, 128), F32),
        pltpu.SemaphoreType.DMA((N_SEMS,)),
        pltpu.SemaphoreType.DMA((N_SEMS,)),
    ]
    grad, loss = pl.pallas_call(
        kernel,
        out_shape=(
            jax.ShapeDtypeStruct((CHUNKS * HALF, FB), F32),
            jax.ShapeDtypeStruct((1, 1), F32),
        ),
        in_specs=[hbm, hbm, smem, vmem, vmem, hbm, hbm, hbm, hbm],
        out_specs=(vmem, vmem),
        scratch_shapes=scratch,
        compiler_params=pltpu.CompilerParams(
            collective_id=0, has_side_effects=True, vmem_limit_bytes=56 * 1024 * 1024
        ),
    )(
        hidden_in.reshape(CHUNKS, HALF, FB),
        teacher_rows.reshape(NX, CAP, FB),
        send_counts.reshape(1, NX),
        doc_ids.reshape(1, CHUNKS * HALF),
        final_gain.reshape(1, FB),
        layer_gain,
        gate_proj,
        up_proj,
        down_proj,
    )
    return grad[None], loss


def solution(mesh):
    in_specs = (
        P("section", "dp", "mp"),
        P(None, "section", None),
        P(None, "section", "dp", "mp"),
        P(None, "section", "dp", "mp"),
        P(None, "section", "mp", "dp"),
        P("mp"),
        P("section", "dp", None, "mp"),
        P("section", "dp", None),
        P("section", "dp", None),
    )
    out_specs = (P("section", "dp", "mp"), P("section", "dp"))
    return jax.shard_map(body, mesh=mesh, in_specs=in_specs, out_specs=out_specs, check_vma=False)
```

```python
import functools

import jax
import jax.numpy as jnp
from jax import lax
from jax.experimental import pallas as pl
from jax.experimental.pallas import tpu as pltpu
from jax.sharding import PartitionSpec as P

D = 8192
DOCS = 8
EPSILON = 1e-05
NX, NY, NZ = 4, 4, 8
CHUNKS = 6
HALF = 96 // CHUNKS
ROWS = NX * HALF
CAP = 48
FB = 256
FF_LOCAL = 512
DB = 2048
EXTRA = 128
PCOLS = 2 * FF_LOCAL + EXTRA
N_SEMS = 400
MESH = pl.DeviceIdType.MESH
ORDER = "0120314023512043152045314250312043516"
ORDER += "243051420512041352430415325403532145"
LAG = 7
F32 = jnp.float32
BF16 = jnp.bfloat16


class Link:
    def __init__(self, send_sems, recv_sems):
        self.send_sems, self.recv_sems = send_sems, recv_sems
        self.used = 0
        self.sent = []
        self.drained = 0

    def take(self, count=1):
        first = self.used
        self.used += count
        return first

    def make(self, src, dst, peer, send, recv):
        return pltpu.make_async_remote_copy(
            src_ref=src,
            dst_ref=dst,
            send_sem=self.send_sems.at[send],
            recv_sem=self.recv_sems.at[recv],
            device_id=peer,
            device_id_type=MESH,
        )

    def put(self, src, dst, peer):
        i = self.take()
        copy = self.make(src, dst, peer, i, i)
        copy.start()
        self.sent.append((None, copy))
        return copy

    def put_if(self, needed, src, dst, peer, send, recv):
        copy = self.make(src, dst, peer, send, recv)
        pl.when(needed)(lambda: copy.start())
        self.sent.append((needed, copy))

    def local(self, src, dst):
        copy = pltpu.make_async_copy(src, dst, self.recv_sems.at[self.take()])
        copy.start()
        return copy

    def drain(self, upto):
        while self.drained < upto:
            needed, copy = self.sent[self.drained]
            self.drained += 1
            if needed is None:
                copy.wait_send()
            else:
                pl.when(needed)(lambda copy=copy: copy.wait_send())


def drive(order, gens, link):
    marks = []
    for name in order:
        if len(marks) > LAG:
            link.drain(marks[-1 - LAG])
        next(gens[int(name)], None)
        marks.append(len(link.sent))
    for gen in gens:
        assert next(gen, "end") == "end"


def kernel(
    hid, tea, cnt, ids, fg, lg, gate, up, down,
    out, loss,
    w1, w2, gains, xs, xn, parts, part_r, inn, terms,
    y_r, z_r, kept, last_r,
    tea_r, cnt_s, cnt_r, targets, weights, final, sum_y, sum_z,
    send_sems, recv_sems,
):
    s = lax.axis_index("section")
    x = lax.axis_index("dp")
    m = lax.axis_index("mp")
    y, z = lax.rem(m, NY), lax.div(m, NY)
    a, b = lax.div(z, 2), lax.rem(z, 2)
    o = 1 - s
    link = Link(send_sems, recv_sems)

    def at_y(k):
        return lax.rem(y + k + NY, NY)

    def at_z(k):
        return lax.rem(z + k + NZ, NZ)

    def at_x(k):
        return lax.rem(x + k + NX, NX)

    def peer_y(k):
        return {"mp": z * NY + at_y(k)}

    def peer_z(k):
        return {"mp": at_z(k) * NY + y}

    def peer_x(k):
        return {"dp": at_x(k)}

    core = {"section": o}
    swap = {"dp": a, "mp": (2 * x + b) * NY + y}
    own_side = a == x
    planes = [{"dp": a, "mp": j * NY + y} for j in range(NZ)]
    homes = [{"dp": j // 2, "mp": (2 * x + j % 2) * NY + y} for j in range(NZ)]

    def other(j):
        return jnp.logical_not(jnp.logical_and(own_side, z == j))

    barrier = pltpu.get_barrier_semaphore()
    peers = (
        [peer_y(k) for k in range(1, NY)]
        + [peer_z(k) for k in range(1, NZ)]
        + [peer_x(k) for k in range(1, NX)]
        + [core]
    )
    for group in (homes, planes):
        for j, peer in enumerate(group):

            @pl.when(other(j))
            def _():
                pl.semaphore_signal(barrier, inc=1, device_id=peer, device_id_type=MESH)

    for peer in peers:
        pl.semaphore_signal(barrier, inc=1, device_id=peer, device_id_type=MESH)

    loads = [
        link.local(gate.at[0, 0], w1.at[s, :, pl.ds(0, FF_LOCAL)]),
        link.local(up.at[0, 0], w1.at[s, :, pl.ds(FF_LOCAL, FF_LOCAL)]),
        link.local(down.at[0, 0], w2.at[s]),
        link.local(lg.at[0, :, pl.ds(pl.multiple_of(x * DB, DB), DB)], gains.at[s]),
    ]
    many = len(peers) + 2 * NZ
    pl.semaphore_wait(barrier, jnp.where(own_side, many - 2, many))

    def spread(group, src, dst, key):
        first = link.take(NZ)
        for j in range(NZ):
            link.put_if(other(j), src(j), dst, group[j], first + j, first + key)
        return first

    def collect(first, ref):
        for j in range(NZ):
            copy = link.make(ref, ref, swap, first + j, first + j)
            pl.when(other(j))(lambda copy=copy: copy.wait_recv())


    def order(n):
        return sorted(range(1, n), key=lambda k: -min(k, n - k))

    def gather_direct(block, pos, peer, n):
        mine = block(pos(0))
        copies = [link.put(mine, mine, peer(k)) for k in order(n)]
        yield
        for copy in copies:
            copy.wait_recv()

    def scatter_direct(block, pos, peer, n, slot, finish):
        copies = [link.put(block(pos(k)), slot(k - 1), peer(k)) for k in order(n)]
        yield
        for copy in copies:
            copy.wait_recv()
        finish(block(pos(0)), [slot(k - 1) for k in range(1, n)])


    def widen(l, c):
        squares = jnp.zeros((ROWS, 128), F32)
        for k in range(8):
            kb, ky = divmod(k, NY)
            value = xs[l, c, kb, ky].reshape(ROWS, FB).astype(F32)
            xn[:, k * FB:(k + 1) * FB] = (value * gains[l, :, k * FB:(k + 1) * FB]).astype(BF16)
            square = value * value
            squares = squares + square[:, :128] + square[:, 128:]
        return jnp.sum(squares, axis=-1, keepdims=True)

    def split_sum(total):
        wide = jnp.broadcast_to(total, total.shape[:-1] + (EXTRA,))
        head = wide.astype(BF16).astype(F32)
        lane = lax.broadcasted_iota(jnp.int32, wide.shape, wide.ndim - 1)
        return jnp.where(lane < EXTRA // 2, head, wide - head).astype(BF16)

    def join_sum(tile):
        return jnp.sum(tile.astype(F32), axis=-1, keepdims=True) * (2.0 / EXTRA)

    def gate_up(l, c):
        extra = split_sum(widen(l, c)).reshape(NX, HALF, EXTRA)
        parts[l, c, :, :, 2 * FF_LOCAL:] = extra
        for n in range(4):
            value = jnp.dot(xn[...], w1[l, :, n * FB:(n + 1) * FB], preferred_element_type=F32)
            parts[l, c, :, :, n * FB:(n + 1) * FB] = value.astype(BF16).reshape(NX, HALF, FB)

    def reduce_parts(l, c):
        def finish(mine, others):
            every = [mine] + others
            squares = sum(join_sum(ref[:, 2 * FF_LOCAL:]) for ref in every)
            scale = lax.rsqrt(squares / D + EPSILON)

            def total(first):
                return sum(ref[:, first:first + FF_LOCAL].astype(F32) for ref in every) * scale

            act = total(0)
            inn[l, c, x] = (act / (1.0 + jnp.exp(-act)) * total(FF_LOCAL)).astype(BF16)

        yield from scatter_direct(
            lambda q: parts.at[l, c, q], at_x, peer_x, NX, lambda i: part_r.at[l, c, i], finish
        )

    def down_terms(l, c):
        rows = inn[l, c].reshape(ROWS, FF_LOCAL)
        for n in range(8):
            nb, ny = divmod(n, NY)
            value = jnp.dot(rows, w2[l, :, n * FB:(n + 1) * FB], preferred_element_type=F32)
            terms[l, c, nb, ny] = value.astype(BF16).reshape(NX, HALF, FB)

    def add_up(mine, others):
        return sum((ref[...].astype(F32) for ref in others), mine[...].astype(F32))

    def sum_terms(mine, others):
        mine[...] = add_up(mine, others).astype(BF16)

    def chain(c):
        landing = xs.at[0, c, b, y, x]
        first = spread(planes, lambda j: hid.at[c], landing, 2 * x + b)

        here = pltpu.make_async_copy(hid.at[c], landing, recv_sems.at[link.take()])
        pl.when(own_side)(lambda: here.start())
        yield
        pl.when(own_side)(lambda: here.wait())
        collect(first, landing)
        for l in range(2):
            if l == 1:
                yield from gather_direct(
                    lambda q: xs.at[1, c, lax.rem(q, 2), y, lax.div(q, 2)], at_z, peer_z, NZ
                )
            yield from gather_direct(lambda q: xs.at[l, c, :, q], at_y, peer_y, NY)
            if l == 0 and c == 0:
                for copy in loads:
                    copy.wait()
                for copy in crossing:
                    copy.wait_recv()
            gate_up(l, c)
            yield from reduce_parts(l, c)
            yield from gather_direct(lambda q: inn.at[l, c, q], at_x, peer_x, NX)
            down_terms(l, c)
            yield from scatter_direct(
                lambda q: terms.at[l, c, :, q], at_y, peer_y, NY, lambda i: y_r.at[l, c, i], sum_terms
            )
            if l == 0:
                def finish(mine, others):
                    fresh = xs[0, c, b, y, a].astype(F32) + add_up(mine, others)
                    xs[1, c, b, y, a] = fresh.astype(BF16)

                yield from scatter_direct(
                    lambda q: terms.at[0, c, lax.rem(q, 2), y, lax.div(q, 2)],
                    at_z, peer_z, NZ, lambda i: z_r.at[c, i], finish,
                )
                base = link.take()
                link.put_if(
                    jnp.logical_not(own_side), xs.at[1, c, b, y, a], kept.at[c], swap, base, base
                )
                state_sems[c] = base

                @pl.when(own_side)
                def _():
                    kept[c] = xs[1, c, b, y, a]

        first = spread(homes, lambda j: terms.at[1, c, j % 2, y, j // 2], last_r.at[c, z], z)

        @pl.when(own_side)
        def _():
            last_r[c, z] = terms[1, c, b, y, a]

        yield
        collect(first, last_r.at[c, 0])
        copy = link.make(kept.at[c], kept.at[c], swap, state_sems[c], state_sems[c])
        pl.when(jnp.logical_not(own_side))(lambda: copy.wait_recv())
        value = kept[c].astype(F32)
        for j in range(NZ):
            value = value + last_r[c, j].astype(F32)
        value = value.astype(BF16).astype(F32)
        final[c * HALF:(c + 1) * HALF] = value
        gained = value * fg[...]
        wanted = targets[c * HALF:(c + 1) * HALF]
        for i, product in enumerate((value * value, gained * gained, gained * wanted, wanted * wanted)):
            sums_of[i].append(as_row(jnp.sum(product, axis=1, keepdims=True), c * HALF))

    n_rows = CHUNKS * HALF
    state_sems, sums_of = [None] * CHUNKS, [[] for _ in range(4)]
    diagonal = lax.broadcasted_iota(jnp.int32, (n_rows, n_rows), 0) == lax.broadcasted_iota(
        jnp.int32, (n_rows, n_rows), 1
    )

    def as_row(column, first):
        shape = (column.shape[0], n_rows)
        own = lax.broadcasted_iota(jnp.int32, shape, 0) + first == lax.broadcasted_iota(jnp.int32, shape, 1)
        return jnp.sum(jnp.where(own, column, 0.0), axis=0, keepdims=True)

    def as_column(line):
        return jnp.sum(jnp.where(diagonal, line, 0.0), axis=1, keepdims=True)

    def prepare():
        own_rows.wait()
        for copy in arrivals:
            copy.wait_recv()
        row = lax.broadcasted_iota(jnp.int32, (n_rows, CAP), 0)
        slot = lax.broadcasted_iota(jnp.int32, (n_rows, CAP), 1)
        start = jnp.zeros((1, CAP), jnp.int32)
        value = jnp.zeros((n_rows, FB), F32)
        for q in range(NX):
            count = cnt_r[q, 0:1, :CAP]
            chosen = jnp.logical_and(row - start == slot, slot < count)
            value += jnp.dot(chosen.astype(BF16), tea_r[q], preferred_element_type=F32)
            start = start + count
        targets[...] = value
        ids_row = ids[...].astype(F32)
        size = jnp.sum((as_column(ids_row) == ids_row).astype(F32), axis=1, keepdims=True)
        weights[...] = jnp.broadcast_to(1.0 / size, weights.shape)
        yield


    chains = [chain(c) for c in range(CHUNKS)]
    for gen in chains:
        next(gen)

    gain_block = lg.at[0, :, pl.ds(pl.multiple_of(x * DB, DB), DB)]
    crossing = [
        link.put(gain_block, gains.at[s], core),
        link.put(gate.at[0, 0], w1.at[s, :, pl.ds(0, FF_LOCAL)], core),
        link.put(up.at[0, 0], w1.at[s, :, pl.ds(FF_LOCAL, FF_LOCAL)], core),
        link.put(down.at[0, 0], w2.at[s], core),
    ]

    for p in range(NX):
        cnt_s[p] = jnp.full((8, 128), cnt[0, p], jnp.int32)
    arrivals = []
    for k in range(1, NX):
        arrivals.append(link.put(tea.at[at_x(k)], tea_r.at[x], peer_x(k)))
        arrivals.append(link.put(cnt_s.at[at_x(k)], cnt_r.at[x], peer_x(k)))
    own_rows = link.local(tea.at[x], tea_r.at[x])
    cnt_r[x] = cnt_s[x]

    drive(ORDER, chains + [prepare()], link)

    for i, lines in enumerate(sums_of):
        sum_y[y, i:i + 1, :n_rows] = sum(lines)
    before = len(link.sent)
    sent = [link.put(sum_y.at[y], sum_y.at[y], peer_y(k)) for k in range(1, NY)]
    link.drain(before)
    for copy in sent:
        copy.wait_recv()
    sum_z[z] = sum_y[0] + sum_y[1] + sum_y[2] + sum_y[3]
    sent = [link.put(sum_z.at[z], sum_z.at[z], peer_z(k)) for k in range(1, NZ)]
    for copy in sent:
        copy.wait_recv()
    sums = sum_z[0]
    for k in range(1, NZ):
        sums = sums + sum_z[k]
    s1, s2, s3, s4 = [as_column(sums[i:i + 1, :n_rows]) for i in range(4)]
    weight = weights[:, :1]
    gain = fg[...]
    rscale = lax.rsqrt(s1 / D + EPSILON)
    inner_sum = weight * (rscale * rscale * s2 - rscale * s3)
    errors = rscale * rscale * s2 - 2.0 * rscale * s3 + s4
    normal = final[...] * rscale
    d_student = weight * (normal * gain - targets[...])
    out[...] = rscale * (gain * d_student - normal * (inner_sum / D))
    total = jnp.sum(weight * 0.5 * errors, axis=0, keepdims=True) / (DOCS * D)
    loss[...] = total

    link.drain(len(link.sent))


def body(
    hidden_in, layer_gain, gate_proj, up_proj, down_proj, final_gain, teacher_rows, send_counts, doc_ids
):
    vmem = pl.BlockSpec(memory_space=pltpu.VMEM)
    smem = pl.BlockSpec(memory_space=pltpu.SMEM)
    hbm = pl.BlockSpec(memory_space=pl.ANY)
    scratch = [
        pltpu.VMEM((2, DB, 2 * FF_LOCAL), BF16),
        pltpu.VMEM((2, FF_LOCAL, DB), BF16),
        pltpu.VMEM((2, 1, DB), F32),
        pltpu.VMEM((2, CHUNKS, 2, NY, NX, HALF, FB), BF16),
        pltpu.VMEM((ROWS, DB), BF16),
        pltpu.VMEM((2, CHUNKS, NX, HALF, PCOLS), BF16),
        pltpu.VMEM((2, CHUNKS, NX - 1, HALF, PCOLS), BF16),
        pltpu.VMEM((2, CHUNKS, NX, HALF, FF_LOCAL), BF16),
        pltpu.VMEM((2, CHUNKS, 2, NY, NX, HALF, FB), BF16),
        pltpu.VMEM((2, CHUNKS, NY - 1, 2, NX, HALF, FB), BF16),
        pltpu.VMEM((CHUNKS, NZ - 1, HALF, FB), BF16),
        pltpu.VMEM((CHUNKS, HALF, FB), BF16),
        pltpu.VMEM((CHUNKS, NZ, HALF, FB), BF16),
        pltpu.VMEM((NX, CAP, FB), BF16),
        pltpu.VMEM((NX, 8, 128), jnp.int32),
        pltpu.VMEM((NX, 8, 128), jnp.int32),
        pltpu.VMEM((CHUNKS * HALF, FB), F32),
        pltpu.VMEM((CHUNKS * HALF, 128), F32),
        pltpu.VMEM((CHUNKS * HALF, FB), F32),
        pltpu.VMEM((NY, 8, 128), F32),
        pltpu.VMEM((NZ, 8, 128), F32),
        pltpu.SemaphoreType.DMA((N_SEMS,)),
        pltpu.SemaphoreType.DMA((N_SEMS,)),
    ]
    grad, loss = pl.pallas_call(
        kernel,
        out_shape=(
            jax.ShapeDtypeStruct((CHUNKS * HALF, FB), F32),
            jax.ShapeDtypeStruct((1, 1), F32),
        ),
        in_specs=[hbm, hbm, smem, vmem, vmem, hbm, hbm, hbm, hbm],
        out_specs=(vmem, vmem),
        scratch_shapes=scratch,
        compiler_params=pltpu.CompilerParams(
            collective_id=0, has_side_effects=True, vmem_limit_bytes=56 * 1024 * 1024
        ),
    )(
        hidden_in.reshape(CHUNKS, HALF, FB),
        teacher_rows.reshape(NX, CAP, FB),
        send_counts.reshape(1, NX),
        doc_ids.reshape(1, CHUNKS * HALF),
        final_gain.reshape(1, FB),
        layer_gain,
        gate_proj,
        up_proj,
        down_proj,
    )
    return grad[None], loss


def solution(mesh):
    in_specs = (
        P("section", "dp", "mp"),
        P(None, "section", None),
        P(None, "section", "dp", "mp"),
        P(None, "section", "dp", "mp"),
        P(None, "section", "mp", "dp"),
        P("mp"),
        P("section", "dp", None, "mp"),
        P("section", "dp", None),
        P("section", "dp", None),
    )
    out_specs = (P("section", "dp", "mp"), P("section", "dp"))
    return jax.shard_map(body, mesh=mesh, in_specs=in_specs, out_specs=out_specs, check_vma=False)
```
